32 devices in a mesh: row: 8 (over z, core), col: 4 (over y, x).
Axes of the slice: x: 2, y: 2, z: 4, core: 2. Of those that a mesh axis runs over, the one named last changes fastest.
Arguments:
- die_current: float32 [16, 1024, 1024], P(None, 'row', 'col')
- die_shunt: float32 [1024, 1024], P('row', 'col'), may hold values from 0.01 to 0.1
- pkg_current: float32 [16, 4096], P(None, ('row', 'col')), may hold values from -6 to 6
- pkg_matrix: float32 [4096, 4096], P('row', 'col'), as said below
- pkg_block_inv: float32 [128, 32, 32], P(('row', 'col')), as said below
- bump_node: int32 [4096], replicated, may hold values from 0 to 1048575, as said below
- bump_conductance: float32 [4096], replicated, may hold values from 0.5 to 4
Outputs:
- die_drop: float32 [16, 1024, 1024], P(None, 'row', 'col')
- package_drop: float32 [16, 4096], P(None, ('row', 'col'))
The draws below stay inside these ranges and needn't reach their ends.
Inputs may be any that keep to these rules, and one draw needn't show every extreme that they name: `bump_node`: bump b lies in lattice cell (b // 64, b % 64) of the die, the cells being 16 rows by 16 columns; the entry is row * 1024 + column, so no two bumps share a node. `pkg_matrix`: symmetric positive definite. `pkg_block_inv`: each block is symmetric positive definite.
All inputs are finite; a program needn't handle non-finite values.
Results may differ from the reference program's by a relative error of at most 0.0003.
Values sent between devices are 32-bit elements; how exact they have to be, the bound alone decides.
A program may use at most 128 MiB of HBM per device.

```python
import math
import jax
import jax.numpy as jnp
from jax import lax

K = 16
NB = 4096
BUMP_C = 64
PB = 32
ITERS = 3
BUMP_R = 64
NX = 1024
NY = 1024


def draw_die_current(key, part):
    rows = jnp.arange(NX, dtype=jnp.float32) / NX
    cols = jnp.arange(NY, dtype=jnp.float32) / NY
    scale = (0.5 + 1.5 * rows)[:, None] * (0.7 + 0.7 * cols)[None, :]
    return jax.random.normal(jax.random.fold_in(key, 12), (K, NX, NY), jnp.float32) * scale


def draw_pkg_matrix(key, part):
    raw = jax.random.normal(jax.random.fold_in(key, 21), (NB, NB), jnp.float32)
    off = (raw + raw.T) / jnp.sqrt(2.0 * NB)
    diag = jax.random.uniform(jax.random.fold_in(key, 22), (NB,), jnp.float32, 4.0, 8.0)
    return off + jnp.diag(diag)


def draw_pkg_block_inv(key, part):
    count = NB // PB
    raw = jax.random.normal(jax.random.fold_in(key, 31), (count, PB, PB), jnp.float32)
    sym = (raw + jnp.swapaxes(raw, 1, 2)) / jnp.sqrt(2.0) * (0.05 / jnp.sqrt(1.0 * PB))
    diag = jax.random.uniform(jax.random.fold_in(key, 32), (count, PB), jnp.float32, 0.15, 0.35)
    return sym + diag[:, :, None] * jnp.eye(PB, dtype=jnp.float32)[None, :, :]


def draw_bump_node(key, part):
    cell_rows = NX // BUMP_R
    cell_cols = NY // BUMP_C
    row_off = jax.random.randint(jax.random.fold_in(key, 41), (NB,), 0, cell_rows)
    col_off = jax.random.randint(jax.random.fold_in(key, 42), (NB,), 0, cell_cols)
    ids = jnp.arange(NB, dtype=jnp.int32)
    grid_row = ids // BUMP_C * cell_rows + row_off
    grid_col = ids % BUMP_C * cell_cols + col_off
    return (grid_row * NY + grid_col).astype(jnp.int32)


def block_levels(own_key, shape, pieces, least, top_value):
    loudness = 1.0
    for position, parts in pieces:
        heights = jax.random.uniform(jax.random.fold_in(jax.random.fold_in(own_key, 6), position), (parts,), jnp.float32, least / len(pieces), top_value / len(pieces))
        loudness = loudness * jnp.repeat(jnp.exp(heights), shape[position] // parts).reshape((-1,) + (1,) * (len(shape) - 1 - position))
    return loudness


def normal_values(rng, dims, width, most, shards=(), kind=jnp.bfloat16):
    gain = block_levels(rng, dims, shards, -0.22, 0.18) if shards else 1.0
    entries = jax.random.normal(rng, dims, jnp.float32) * width * gain
    return jnp.minimum(jnp.maximum(entries, -most), most).astype(kind)


def setup_inputs(seed: int = 0) -> dict:
    key_list = jax.random.split(jax.random.key(seed), 8)
    die_current = draw_die_current(jax.random.fold_in(key_list[7], 71), 0)
    die_shunt = jnp.clip(jnp.exp(math.log(0.1) - 2.3025851 * jax.random.uniform(key_list[1], (NX, NY), jnp.float32) ** block_levels(key_list[1], (NX, NY), ((0, 8), (1, 4)), -0.2, 0.2)), 0.01, 0.1)
    pkg_current = normal_values(key_list[2], (K, NB), 1.0, 6.0, ((1, 32),), jnp.float32)
    pkg_matrix = draw_pkg_matrix(jax.random.fold_in(key_list[7], 71), 0)
    pkg_block_inv = draw_pkg_block_inv(jax.random.fold_in(key_list[7], 71), 0)
    bump_node = draw_bump_node(jax.random.fold_in(key_list[7], 71), 0)
    bump_conductance = jnp.clip(jnp.exp(jax.random.uniform(key_list[6], (NB,), jnp.float32, math.log(0.5), math.log(4.0))), 0.5, 4.0)
    return dict(die_current=die_current, die_shunt=die_shunt, pkg_current=pkg_current, pkg_matrix=pkg_matrix, pkg_block_inv=pkg_block_inv, bump_node=bump_node, bump_conductance=bump_conductance)


def laplace(field, shunt):
    padded = jnp.pad(field, ((0, 0), (1, 1), (1, 1)))
    beside_all = padded[:, 2:, 1:-1] + padded[:, :-2, 1:-1]
    beside_all = beside_all + padded[:, 1:-1, 2:] + padded[:, 1:-1, :-2]
    return (4.0 + shunt) * field - beside_all


def reference(die_current, die_shunt, pkg_current, pkg_matrix, pkg_block_inv, bump_node, bump_conductance):
    rows_b = (bump_node // NY).astype(jnp.int32)
    cols_b = (bump_node % NY).astype(jnp.int32)
    diag_die = (4.0 + die_shunt).at[rows_b, cols_b].add(bump_conductance)

    def apply_op(vd, vp):
        at_bumps = vd[:, rows_b, cols_b]
        die = laplace(vd, die_shunt).at[:, rows_b, cols_b].add(bump_conductance * (at_bumps - vp))
        prod = lax.dot_general(vp, pkg_matrix, (((1,), (1,)), ((), ())), precision=lax.Precision.HIGHEST)
        return die, prod + bump_conductance * (vp - at_bumps)

    def precond(rd, rp):
        blocks = rp.reshape(rp.shape[0], -1, PB)
        zp = jnp.einsum("bac,kbc->kba", pkg_block_inv, blocks, precision=lax.Precision.HIGHEST)
        return rd / diag_die, zp.reshape(rp.shape)

    def inner(ad, ap, bd, bp):
        return jnp.sum(ad * bd, axis=(1, 2)) + jnp.sum(ap * bp, axis=1)

    xd = jnp.zeros_like(die_current)
    xp = jnp.zeros_like(pkg_current)
    rd, rp = die_current, pkg_current
    zd, zp = precond(rd, rp)
    pd, pp = zd, zp
    rz = inner(rd, rp, zd, zp)
    for step in range(ITERS):
        qd, qp = apply_op(pd, pp)
        alpha = rz / inner(pd, pp, qd, qp)
        xd = xd + alpha[:, None, None] * pd
        xp = xp + alpha[:, None] * pp
        rd = rd - alpha[:, None, None] * qd
        rp = rp - alpha[:, None] * qp
        zd, zp = precond(rd, rp)
        fresh = inner(rd, rp, zd, zp)
        ratio = fresh / rz
        pd = zd + ratio[:, None, None] * pd
        pp = zp + ratio[:, None] * pp
        rz = fresh
    return xd, xp
```

```python
import functools

import jax
import jax.numpy as jnp
from jax import lax
from jax.experimental import pallas as pl
from jax.experimental.pallas import tpu as pltpu
from jax.sharding import PartitionSpec as P

BUMP_C = 64
PB = 32
ITERS = 3
MESH = pl.DeviceIdType.MESH
HI = lax.Precision.HIGHEST
F32 = jnp.float32


def drain(ref, sem):
    pltpu.make_async_copy(ref, ref, sem).wait()


def kernel(
    nrows, ncols, lat_rows, lat_cols,
    rd_ref, shunt_ref, rp_ref, mat_ref, inv_ref, locr_ref, locc_ref, cexp_ref, chere_ref,
    xd_ref, xp_ref,
    us, ws, rbuf, diag, invd, mask, cmask, mh, ml, bd, gbuf, dbuf, cf, abuf, vpx,
    rsend, hr, csend, hc, seg, part, rec, cont, dat, red,
    hsend, hrecv, ssend, srecv, psend, precv, csendm, drecv, rsendm, rrecv, selfsem,
):
    ndev = nrows * ncols
    irow = lax.axis_index("row")
    icol = lax.axis_index("col")
    me = irow * ncols + icol
    batch, tile_r, tile_c = rd_ref.shape
    local_n = rp_ref.shape[1]
    cell_r = tile_r // lat_rows
    cell_c = tile_c // lat_cols

    hr[...] = jnp.zeros_like(hr)
    hc[...] = jnp.zeros_like(hc)
    barrier = pltpu.get_barrier_semaphore()

    def greet(d, c):
        t = lax.rem(me + d, ndev)
        pl.semaphore_signal(
            barrier, inc=1, device_id=(t // ncols, lax.rem(t, ncols)), device_id_type=MESH
        )
        return c

    lax.fori_loop(1, ndev, greet, 0)

    row_c = lax.broadcasted_iota(jnp.int32, (cell_r, tile_c), 0)
    lane_c = lax.rem(lax.broadcasted_iota(jnp.int32, (cell_r, tile_c), 1), cell_c)
    for lr in range(lat_rows):
        rs = slice(lr * cell_r, (lr + 1) * cell_r)
        hit = (row_c == locr_ref[lr : lr + 1, :]) & (lane_c == locc_ref[lr : lr + 1, :])
        m = jnp.where(hit, 1.0, 0.0)
        cm = m * cexp_ref[lr : lr + 1, :]
        mask[rs, :] = m
        cmask[rs, :] = cm
        dg = 4.0 + shunt_ref[rs, :] + cm
        diag[rs, :] = dg
        invd[rs, :] = 1.0 / dg
    bd[...] = jnp.zeros_like(bd)
    for q in range(local_n // PB):
        bd[q * PB : (q + 1) * PB, q * PB : (q + 1) * PB] = inv_ref[q]
    high = mat_ref[...].astype(jnp.bfloat16)
    mh[...] = high
    ml[...] = (mat_ref[...] - high.astype(F32)).astype(jnp.bfloat16)

    node_c = icol * lat_cols + lax.broadcasted_iota(jnp.int32, (tile_c, local_n), 0) // cell_c
    node_l = lax.broadcasted_iota(jnp.int32, (tile_c, local_n), 1)
    embeds = {}

    def embed(lr, j):
        off = lr * BUMP_C - j * local_n
        if off not in embeds:
            embeds[off] = jnp.where(node_c + off == node_l, 1.0, 0.0)
        return embeds[off]

    def meets(lr, j):
        return lr * BUMP_C < (j + 1) * local_n and j * local_n < (lr + 1) * BUMP_C

    lane_e = lax.broadcasted_iota(jnp.int32, (tile_r, 128), 1)
    row_i = lax.broadcasted_iota(jnp.int32, (tile_r, tile_c), 0)
    lane_i = lax.broadcasted_iota(jnp.int32, (tile_r, tile_c), 1)
    sub_k = lax.broadcasted_iota(jnp.int32, (batch, 128), 0)
    lane_k = lax.broadcasted_iota(jnp.int32, (batch, 128), 1)

    def remote(src, dst, ssem, rsem, r, c):
        return pltpu.make_async_remote_copy(
            src_ref=src, dst_ref=dst, send_sem=ssem, recv_sem=rsem,
            device_id=(r, c), device_id_type=MESH,
        )

    has = (irow > 0, irow < nrows - 1, icol > 0, icol < ncols - 1)

    def halos(it):
        return (
            remote(rsend.at[it, 0], hr.at[it, 1], hsend.at[it, 0], hrecv.at[it, 1], irow - 1, icol),
            remote(rsend.at[it, 1], hr.at[it, 0], hsend.at[it, 1], hrecv.at[it, 0], irow + 1, icol),
            remote(csend.at[it, 0], hc.at[it, 1], hsend.at[it, 2], hrecv.at[it, 3], irow, icol - 1),
            remote(csend.at[it, 1], hc.at[it, 0], hsend.at[it, 3], hrecv.at[it, 2], irow, icol + 1),
        )

    def put(slot, value):
        cf[slot] = jnp.broadcast_to(value, (batch, tile_c))

    rp = rp_ref[...]
    ups, gs, sp, alphas, betas = [], [], None, [], []
    chere = chere_ref[...]

    for it in range(ITERS):
        up = lax.dot_general(rp, bd[...], (((1,), (1,)), ((), ())), precision=HI)
        ups.append(up)
        seg[it, icol] = up
        if it == 0:
            pl.semaphore_wait(barrier, ndev - 1)
        for d in range(1, ncols):
            remote(
                seg.at[it, icol], seg.at[it, icol], ssend.at[it], srecv.at[it],
                irow, lax.rem(icol + d, ncols),
            ).start()

        def phase_u(k, e):
            one = pl.ds(k, 1)
            if it == 0:
                r = rd_ref[k]
            elif it == 1:
                r = rd_ref[k] - cf[0, one, :] * ws[0, k]
                rbuf[k] = r
            else:
                r = rbuf[k] - (cf[1, one, :] * ws[1, k] + cf[2, one, :] * ws[0, k])
            u = r * invd[...]
            us[it, k] = u
            gbuf[one, :] = jnp.sum(r * u, axis=0, keepdims=True)
            rsend[it, 0, one, :] = u[0:1, :]
            rsend[it, 1, one, :] = u[tile_r - 1 : tile_r, :]
            mu = u * mask[...]
            for lr in range(lat_rows):
                abuf[lr, one, :] = jnp.sum(
                    mu[lr * cell_r : (lr + 1) * cell_r], axis=0, keepdims=True
                )
            e = jnp.where(lane_e == k, u[:, 0:1], e)
            return jnp.where(lane_e == k + batch, u[:, tile_c - 1 : tile_c], e)

        e = lax.fori_loop(0, batch, phase_u, jnp.zeros((tile_r, 128), F32))
        et = e.T
        csend[it, 0] = et[0:batch, :]
        csend[it, 1] = et[batch : 2 * batch, :]
        for side, copy in enumerate(halos(it)):
            pl.when(has[side])(copy.start)
        for j in range(ncols):
            total = jnp.zeros((batch, local_n), F32)
            for lr in range(lat_rows):
                if meets(lr, j):
                    total += jnp.dot(abuf[lr], embed(lr, j), precision=HI)
            cont[it, j] = total
        dat[it, icol] = cont[it, icol]
        for d in range(1, ncols):
            t = lax.rem(icol + d, ncols)
            remote(
                cont.at[it, t], dat.at[it, icol], csendm.at[it], drecv.at[it], irow, t
            ).start()

        drain(seg.at[it, 0 : ncols - 1], srecv.at[it])
        acc = None
        for j in range(ncols):
            v = seg[it, j]
            vh = v.astype(jnp.bfloat16)
            vl = (v - vh.astype(F32)).astype(jnp.bfloat16)
            ks = slice(j * local_n, (j + 1) * local_n)
            both = jnp.dot(
                jnp.concatenate([vh, vl], axis=0), mh[ks, :], preferred_element_type=F32
            )
            term = both[:batch] + both[batch:]
            term += jnp.dot(vh, ml[ks, :], preferred_element_type=F32)
            acc = term if acc is None else acc + term
        for m in range(nrows):
            part[it, m] = acc[:, m * local_n : (m + 1) * local_n]
        for m in range(nrows):
            n = icol * nrows + m
            copy = remote(
                part.at[it, m], rec.at[it, irow], psend.at[it], precv.at[it],
                n // ncols, lax.rem(n, ncols),
            )
            pl.when(n != me)(copy.start)

            @pl.when(n == me)
            def _():
                pltpu.make_async_copy(part.at[it, m], rec.at[it, irow], precv.at[it]).start()

        for lr in range(lat_rows):
            total = jnp.zeros((batch, tile_c), F32)
            for j in range(ncols):
                if meets(lr, j):
                    total += lax.dot_general(
                        seg[it, j], embed(lr, j), (((1,), (1,)), ((), ())), precision=HI
                    )
            vpx[lr] = total

        for side, index in enumerate(((hr, 0), (hr, 1), (hc, 0), (hc, 1))):
            ref, pos = index

            @pl.when(has[side])
            def _():
                drain(ref.at[it, pos], hrecv.at[it, side])

        ct = jnp.concatenate(
            [hc[it, 0], hc[it, 1], jnp.zeros((128 - 2 * batch, tile_r), F32)], axis=0
        ).T

        def phase_w(k, c):
            one = pl.ds(k, 1)
            u = us[it, k]
            left = jnp.sum(jnp.where(lane_e == k, ct, 0.0), axis=1, keepdims=True)
            right = jnp.sum(jnp.where(lane_e == k + batch, ct, 0.0), axis=1, keepdims=True)
            near = jnp.where(row_i == 0, hr[it, 0, one, :], pltpu.roll(u, 1, 0))
            near += jnp.where(row_i == tile_r - 1, hr[it, 1, one, :], pltpu.roll(u, tile_r - 1, 0))
            near += jnp.where(lane_i == 0, left, pltpu.roll(u, 1, 1))
            near += jnp.where(lane_i == tile_c - 1, right, pltpu.roll(u, tile_c - 1, 1))
            feed = jnp.concatenate(
                [
                    cmask[lr * cell_r : (lr + 1) * cell_r, :] * vpx[lr, one, :]
                    for lr in range(lat_rows)
                ],
                axis=0,
            )
            w = diag[...] * u - near - feed
            if it + 1 < ITERS:
                ws[it, k] = w
            dbuf[one, :] = jnp.sum(w * u, axis=0, keepdims=True)
            return c

        lax.fori_loop(0, batch, phase_w, 0)

        drain(rec.at[it], precv.at[it])
        drain(dat.at[it, 0 : ncols - 1], drecv.at[it])
        qp = rec[it, 0]
        for i in range(1, nrows):
            qp += rec[it, i]
        die_at = dat[it, 0]
        for j in range(1, ncols):
            die_at += dat[it, j]
        qp += chere * (up - die_at)
        g = jnp.sum(gbuf[...], axis=1, keepdims=True) + jnp.sum(rp * up, axis=1, keepdims=True)
        d = jnp.sum(dbuf[...], axis=1, keepdims=True) + jnp.sum(up * qp, axis=1, keepdims=True)
        line = jnp.where(lane_k == sub_k, g, 0.0) + jnp.where(lane_k == sub_k + batch, d, 0.0)
        red[it, me] = jnp.sum(line, axis=0, keepdims=True)

        def spread(d, c):
            t = lax.rem(me + d, ndev)
            remote(
                red.at[it, me], red.at[it, me], rsendm.at[it], rrecv.at[it],
                t // ncols, lax.rem(t, ncols),
            ).start()
            return c

        lax.fori_loop(1, ndev, spread, 0)
        drain(red.at[it, 0 : ndev - 1], rrecv.at[it])
        line = jnp.sum(red[it], axis=0)
        g = jnp.sum(jnp.where(lane_k == sub_k, line, 0.0), axis=1, keepdims=True)
        d = jnp.sum(jnp.where(lane_k == sub_k + batch, line, 0.0), axis=1, keepdims=True)
        if it == 0:
            alpha = g / d
            sp = qp
            put(0, alpha)
        else:
            beta = g / gs[-1]
            betas.append(beta)
            alpha = g / (d - beta * g / alphas[-1])
            sp = qp + beta * sp
            if it == 1:
                put(1, alpha)
                put(2, alpha * beta)
        gs.append(g)
        alphas.append(alpha)
        rp = rp - alpha * sp

    c2 = alphas[2]
    c1 = alphas[1] + c2 * betas[1]
    c0 = alphas[0] + c1 * betas[0]
    put(0, c0)
    put(1, c1)
    put(2, c2)
    xp_ref[...] = c0 * ups[0] + c1 * ups[1] + c2 * ups[2]

    def finish(k, c):
        one = pl.ds(k, 1)
        xd_ref[k] = cf[0, one, :] * us[0, k] + cf[1, one, :] * us[1, k] + cf[2, one, :] * us[2, k]
        return c

    lax.fori_loop(0, batch, finish, 0)

    mine = me // nrows == icol
    for it in range(ITERS):
        drain(seg.at[it, 0 : ncols - 1], ssend.at[it])
        drain(cont.at[it, 0 : ncols - 1], csendm.at[it])
        drain(red.at[it, 0 : ndev - 1], rsendm.at[it])

        @pl.when(mine)
        def _():
            drain(part.at[it, 0 : nrows - 1], psend.at[it])

        @pl.when(jnp.logical_not(mine))
        def _():
            drain(part.at[it], psend.at[it])

        for side, copy in enumerate(halos(it)):
            pl.when(has[side])(copy.wait_send)


def solution(mesh):
    nrows, ncols = mesh.shape["row"], mesh.shape["col"]

    def body(die_current, die_shunt, pkg_current, pkg_matrix, pkg_block_inv, bump_node, bump_conductance):
        irow = lax.axis_index("row")
        icol = lax.axis_index("col")
        batch, tile_r, tile_c = die_current.shape
        local_n = pkg_current.shape[1]
        bumps = bump_node.shape[0]
        lat_rows = bumps // BUMP_C // nrows
        lat_cols = BUMP_C // ncols
        cell_r, cell_c = tile_r // lat_rows, tile_c // lat_cols
        total_c = tile_c * ncols
        at = (irow * lat_rows, icol * lat_cols)
        nodes = lax.dynamic_slice(bump_node.reshape(-1, BUMP_C), at, (lat_rows, lat_cols))
        cond = lax.dynamic_slice(bump_conductance.reshape(-1, BUMP_C), at, (lat_rows, lat_cols))
        nodes = jnp.repeat(nodes, cell_c, axis=1)
        cond = jnp.repeat(cond, cell_c, axis=1)
        loc_r = (nodes // total_c) % cell_r
        loc_c = (nodes % total_c) % cell_c
        here = lax.dynamic_slice_in_dim(
            bump_conductance, (irow * ncols + icol) * local_n, local_n
        ).reshape(1, local_n)
        ndev = nrows * ncols
        vm = pltpu.VMEM
        dma = pltpu.SemaphoreType.DMA
        row = (batch, tile_c)
        return pl.pallas_call(
            functools.partial(kernel, nrows, ncols, lat_rows, lat_cols),
            out_shape=(
                jax.ShapeDtypeStruct(die_current.shape, F32),
                jax.ShapeDtypeStruct(pkg_current.shape, F32),
            ),
            in_specs=[pl.BlockSpec(memory_space=pltpu.VMEM)] * 9,
            out_specs=(pl.BlockSpec(memory_space=pltpu.VMEM),) * 2,
            scratch_shapes=[
                vm((ITERS,) + die_current.shape, F32),
                vm((ITERS - 1,) + die_current.shape, F32),
                vm(die_current.shape, F32),
                vm((tile_r, tile_c), F32),
                vm((tile_r, tile_c), F32),
                vm((tile_r, tile_c), F32),
                vm((tile_r, tile_c), F32),
                vm(pkg_matrix.shape, jnp.bfloat16),
                vm(pkg_matrix.shape, jnp.bfloat16),
                vm((local_n, local_n), F32),
                vm(row, F32),
                vm(row, F32),
                vm((3,) + row, F32),
                vm((lat_rows,) + row, F32),
                vm((lat_rows,) + row, F32),
                vm((ITERS, 2) + row, F32),
                vm((ITERS, 2) + row, F32),
                vm((ITERS, 2, batch, tile_r), F32),
                vm((ITERS, 2, batch, tile_r), F32),
                vm((ITERS, ncols, batch, local_n), F32),
                vm((ITERS, nrows, batch, local_n), F32),
                vm((ITERS, nrows, batch, local_n), F32),
                vm((ITERS, ncols, batch, local_n), F32),
                vm((ITERS, ncols, batch, local_n), F32),
                vm((ITERS, ndev, 1, 128), F32),
                dma((ITERS, 4)),
                dma((ITERS, 4)),
                dma((ITERS,)),
                dma((ITERS,)),
                dma((ITERS,)),
                dma((ITERS,)),
                dma((ITERS,)),
                dma((ITERS,)),
                dma((ITERS,)),
                dma((ITERS,)),
                dma((ITERS,)),
            ],
            compiler_params=pltpu.CompilerParams(
                collective_id=0, has_side_effects=True, vmem_limit_bytes=48 << 20
            ),
        )(die_current, die_shunt, pkg_current, pkg_matrix, pkg_block_inv, loc_r, loc_c, cond, here)

    placed = (
        P(None, "row", "col"),
        P("row", "col"),
        P(None, ("row", "col")),
        P("row", "col"),
        P(("row", "col"), None, None),
        P(),
        P(),
    )
    return jax.shard_map(
        body,
        mesh=mesh,
        in_specs=placed,
        out_specs=(P(None, "row", "col"), P(None, ("row", "col"))),
        check_vma=False,
    )
```

```python
import functools

import jax
import jax.numpy as jnp
from jax import lax
from jax.experimental import pallas as pl
from jax.experimental.pallas import tpu as pltpu
from jax.sharding import PartitionSpec as P

BUMP_C = 64
PB = 32
ITERS = 3
MESH = pl.DeviceIdType.MESH
HI = lax.Precision.HIGHEST
F32 = jnp.float32


def drain(ref, sem):
    pltpu.make_async_copy(ref, ref, sem).wait()


def split3(v):
    high = v.astype(jnp.bfloat16)
    rest = v - high.astype(F32)
    mid = rest.astype(jnp.bfloat16)
    return [high, mid, (rest - mid.astype(F32)).astype(jnp.bfloat16)]


def exact_pick(parts, onehot):
    rows = sum(p.shape[0] for p in parts)
    stacked = jnp.concatenate(parts, axis=0) if len(parts) > 1 else parts[0]
    out = jnp.dot(
        jnp.concatenate(split3(stacked), axis=0), onehot, preferred_element_type=F32
    )
    return out[:rows] + out[rows : 2 * rows] + out[2 * rows :]


def pairs_by_offset(lat_rows, ncols, local_n):
    groups = {}
    for lr in range(lat_rows):
        for j in range(ncols):
            if lr * BUMP_C < (j + 1) * local_n and j * local_n < (lr + 1) * BUMP_C:
                groups.setdefault(lr * BUMP_C - j * local_n, []).append((lr, j))
    return sorted(groups.items())


def kernel(
    nrows, ncols, lat_rows, lat_cols,
    rd_hbm, shunt_ref, rp_ref, mat_hbm, inv_ref, node_ref, cond_ref,
    xd_ref, xp_ref,
    rd_ref, mat_ref, us, ms, ks, diag, invd, mask, cinv, mh, ml, bd, gbuf, dbuf, cf, abuf, vpx,
    emb, embt, rsend, hr, csend, hc, seg, part, rec, cont, dat, red,
    hsend, hrecv, ssend, srecv, psend, precv, csendm, drecv, rsendm, rrecv, loadsem,
):
    ndev = nrows * ncols
    irow = lax.axis_index("row")
    icol = lax.axis_index("col")
    me = irow * ncols + icol
    batch, tile_r, tile_c = rd_ref.shape
    local_n = rp_ref.shape[1]
    cell_r = tile_r // lat_rows
    cell_c = tile_c // lat_cols
    total_c = tile_c * ncols
    groups = pairs_by_offset(lat_rows, ncols, local_n)

    load_rd = pltpu.make_async_copy(rd_hbm, rd_ref, loadsem.at[0])
    load_mat = pltpu.make_async_copy(mat_hbm, mat_ref, loadsem.at[1])
    load_rd.start()
    load_mat.start()

    hr[...] = jnp.zeros_like(hr)
    hc[...] = jnp.zeros_like(hc)
    barrier = pltpu.get_barrier_semaphore()

    def greet(d, c):
        t = lax.rem(me + d, ndev)
        pl.semaphore_signal(
            barrier, inc=1, device_id=(t // ncols, lax.rem(t, ncols)), device_id_type=MESH
        )
        return c

    lax.fori_loop(1, ndev, greet, 0)

    seg_rows = lat_rows * BUMP_C // 128
    per_row = 128 // BUMP_C
    nodes = node_ref[pl.ds(irow * seg_rows, seg_rows), :]
    conds = cond_ref[pl.ds(irow * seg_rows, seg_rows), :]
    node_r = lax.rem(nodes // total_c, cell_r).astype(F32)
    node_q = lax.rem(lax.rem(nodes, total_c), cell_c).astype(F32)
    tall = jnp.concatenate([node_r, node_q, conds], axis=0)
    tall = jnp.concatenate([tall, jnp.zeros((-tall.shape[0] % 8, 128), F32)], axis=0)
    wide_l = lax.broadcasted_iota(jnp.int32, (128, tile_c), 0)
    wide_c = lax.broadcasted_iota(jnp.int32, (128, tile_c), 1) // cell_c + icol * lat_cols
    row_c = lax.broadcasted_iota(jnp.int32, (cell_r, tile_c), 0).astype(F32)
    lane_c = lax.rem(lax.broadcasted_iota(jnp.int32, (cell_r, tile_c), 1), cell_c).astype(F32)
    for q in range(per_row):
        pick = jnp.where(wide_l == wide_c + q * BUMP_C, 1.0, 0.0).astype(jnp.bfloat16)
        flat = exact_pick([tall], pick)
        for i in range(seg_rows):
            lr = i * per_row + q
            rs = slice(lr * cell_r, (lr + 1) * cell_r)
            hit = (row_c == flat[i : i + 1, :]) & (
                lane_c == flat[seg_rows + i : seg_rows + i + 1, :]
            )
            m = jnp.where(hit, 1.0, 0.0)
            cm = m * flat[2 * seg_rows + i : 2 * seg_rows + i + 1, :]
            dg = 4.0 + shunt_ref[rs, :] + cm
            iv = 1.0 / dg
            mask[rs, :] = m
            diag[rs, :] = dg
            invd[rs, :] = iv
            cinv[rs, :] = cm * iv
    first = me * local_n
    mine_l = lax.broadcasted_iota(jnp.int32, (128, local_n), 0)
    mine_n = lax.broadcasted_iota(jnp.int32, (128, local_n), 1) + lax.rem(first, 128)
    own = jnp.broadcast_to(cond_ref[pl.ds(first // 128, 1), :], (8, 128))
    chere = exact_pick([own], jnp.where(mine_l == mine_n, 1.0, 0.0).astype(jnp.bfloat16))[0:1]

    bd[...] = jnp.zeros_like(bd)
    for q in range(local_n // PB):
        bd[q * PB : (q + 1) * PB, q * PB : (q + 1) * PB] = inv_ref[q]

    node_c = icol * lat_cols + lax.broadcasted_iota(jnp.int32, (tile_c, local_n), 0) // cell_c
    node_l = lax.broadcasted_iota(jnp.int32, (tile_c, local_n), 1)
    node_ct = icol * lat_cols + lax.broadcasted_iota(jnp.int32, (local_n, tile_c), 1) // cell_c
    node_lt = lax.broadcasted_iota(jnp.int32, (local_n, tile_c), 0)
    for g, (off, members) in enumerate(groups):
        emb[g] = jnp.where(node_c + off == node_l, 1.0, 0.0).astype(jnp.bfloat16)
        embt[g] = jnp.where(node_ct + off == node_lt, 1.0, 0.0).astype(jnp.bfloat16)

    lane_e = lax.broadcasted_iota(jnp.int32, (tile_r, 128), 1)
    row_i = lax.broadcasted_iota(jnp.int32, (tile_r, tile_c), 0)
    lane_i = lax.broadcasted_iota(jnp.int32, (tile_r, tile_c), 1)
    sub_k = lax.broadcasted_iota(jnp.int32, (batch, 128), 0)
    lane_k = lax.broadcasted_iota(jnp.int32, (batch, 128), 1)

    def remote(src, dst, ssem, rsem, r, c):
        return pltpu.make_async_remote_copy(
            src_ref=src, dst_ref=dst, send_sem=ssem, recv_sem=rsem,
            device_id=(r, c), device_id_type=MESH,
        )

    has = (irow > 0, irow < nrows - 1, icol > 0, icol < ncols - 1)

    def halos(it):
        return (
            remote(rsend.at[it, 0], hr.at[it, 1], hsend.at[it, 0], hrecv.at[it, 1], irow - 1, icol),
            remote(rsend.at[it, 1], hr.at[it, 0], hsend.at[it, 1], hrecv.at[it, 0], irow + 1, icol),
            remote(csend.at[it, 0], hc.at[it, 1], hsend.at[it, 2], hrecv.at[it, 3], irow, icol - 1),
            remote(csend.at[it, 1], hc.at[it, 0], hsend.at[it, 3], hrecv.at[it, 2], irow, icol + 1),
        )

    def put(slot, value):
        cf[slot] = jnp.broadcast_to(value, (batch, tile_c))

    def precond(v):
        return lax.dot_general(v, bd[...], (((1,), (1,)), ((), ())), precision=HI)

    def send_seg(it, v):
        seg[it, icol] = v
        for d in range(1, ncols):
            remote(
                seg.at[it, icol], seg.at[it, icol], ssend.at[it], srecv.at[it],
                irow, lax.rem(icol + d, ncols),
            ).start()

    def edges(it, k, v, e):
        one = pl.ds(k, 1)
        rsend[it, 0, one, :] = v[0:1, :]
        rsend[it, 1, one, :] = v[tile_r - 1 : tile_r, :]
        mv = v * mask[...]
        for lr in range(lat_rows):
            abuf[lr, one, :] = jnp.sum(mv[lr * cell_r : (lr + 1) * cell_r], axis=0, keepdims=True)
        e = jnp.where(lane_e == k, v[:, 0:1], e)
        return jnp.where(lane_e == k + batch, v[:, tile_c - 1 : tile_c], e)

    def send_edges(it, e):
        et = e.T
        csend[it, 0] = et[0:batch, :]
        csend[it, 1] = et[batch : 2 * batch, :]
        for side, copy in enumerate(halos(it)):
            pl.when(has[side])(copy.start)

    def send_cont(it):
        totals = [None] * ncols
        for g, (off, members) in enumerate(groups):
            out = exact_pick([abuf[lr] for lr, j in members], emb[g])
            for i, (lr, j) in enumerate(members):
                term = out[i * batch : (i + 1) * batch]
                totals[j] = term if totals[j] is None else totals[j] + term
        for j in range(ncols):
            cont[it, j] = totals[j]
        dat[it, icol] = cont[it, icol]
        for d in range(1, ncols):
            t = lax.rem(icol + d, ncols)
            remote(
                cont.at[it, t], dat.at[it, icol], csendm.at[it], drecv.at[it], irow, t
            ).start()

    def package_product(it):
        drain(seg.at[it, 0 : ncols - 1], srecv.at[it])
        acc = None
        for j in range(ncols):
            v = seg[it, j]
            vh = v.astype(jnp.bfloat16)
            vl = (v - vh.astype(F32)).astype(jnp.bfloat16)
            span = slice(j * local_n, (j + 1) * local_n)
            both = jnp.dot(
                jnp.concatenate([vh, vl], axis=0), mh[span, :], preferred_element_type=F32
            )
            term = both[:batch] + both[batch:]
            term += jnp.dot(vh, ml[span, :], preferred_element_type=F32)
            acc = term if acc is None else acc + term
        for m in range(nrows):
            part[it, m] = acc[:, m * local_n : (m + 1) * local_n]
        for m in range(nrows):
            n = icol * nrows + m
            copy = remote(
                part.at[it, m], rec.at[it, irow], psend.at[it], precv.at[it],
                n // ncols, lax.rem(n, ncols),
            )
            pl.when(n != me)(copy.start)

            @pl.when(n == me)
            def _():
                pltpu.make_async_copy(part.at[it, m], rec.at[it, irow], precv.at[it]).start()

        totals = [None] * lat_rows
        for g, (off, members) in enumerate(groups):
            out = exact_pick([seg[it, j] for lr, j in members], embt[g])
            for i, (lr, j) in enumerate(members):
                term = out[i * batch : (i + 1) * batch]
                totals[lr] = term if totals[lr] is None else totals[lr] + term
        for lr in range(lat_rows):
            vpx[lr] = totals[lr]

    def wait_halos(it):
        for side, index in enumerate(((hr, 0), (hr, 1), (hc, 0), (hc, 1))):
            ref, pos = index

            @pl.when(has[side])
            def _():
                drain(ref.at[it, pos], hrecv.at[it, side])

        return jnp.concatenate(
            [hc[it, 0], hc[it, 1], jnp.zeros((128 - 2 * batch, tile_r), F32)], axis=0
        ).T

    def image(it, k, v, ct):
        one = pl.ds(k, 1)
        left = jnp.sum(jnp.where(lane_e == k, ct, 0.0), axis=1, keepdims=True)
        right = jnp.sum(jnp.where(lane_e == k + batch, ct, 0.0), axis=1, keepdims=True)
        near = jnp.where(row_i == 0, hr[it, 0, one, :], pltpu.roll(v, 1, 0))
        near += jnp.where(row_i == tile_r - 1, hr[it, 1, one, :], pltpu.roll(v, tile_r - 1, 0))
        near += jnp.where(lane_i == 0, left, pltpu.roll(v, 1, 1))
        near += jnp.where(lane_i == tile_c - 1, right, pltpu.roll(v, tile_c - 1, 1))
        feed = jnp.concatenate(
            [
                cinv[lr * cell_r : (lr + 1) * cell_r, :] * vpx[lr, one, :]
                for lr in range(lat_rows)
            ],
            axis=0,
        )
        return v - near * invd[...] - feed

    def package_image(it, v):
        drain(rec.at[it], precv.at[it])
        drain(dat.at[it, 0 : ncols - 1], drecv.at[it])
        out = rec[it, 0]
        for i in range(1, nrows):
            out += rec[it, i]
        die_at = dat[it, 0]
        for j in range(1, ncols):
            die_at += dat[it, j]
        return out + chere * (v - die_at)

    def total(buf, a, b):
        return jnp.sum(buf[...], axis=1, keepdims=True) + jnp.sum(a * b, axis=1, keepdims=True)

    def send_sums(it, g, d):
        line = jnp.where(lane_k == sub_k, g, 0.0) + jnp.where(lane_k == sub_k + batch, d, 0.0)
        red[it, me] = jnp.sum(line, axis=0, keepdims=True)

        def spread(d, c):
            t = lax.rem(me + d, ndev)
            remote(
                red.at[it, me], red.at[it, me], rsendm.at[it], rrecv.at[it],
                t // ncols, lax.rem(t, ncols),
            ).start()
            return c

        lax.fori_loop(1, ndev, spread, 0)

    def take_sums(it):
        drain(red.at[it, 0 : ndev - 1], rrecv.at[it])
        line = jnp.sum(red[it], axis=0)
        g = jnp.sum(jnp.where(lane_k == sub_k, line, 0.0), axis=1, keepdims=True)
        d = jnp.sum(jnp.where(lane_k == sub_k + batch, line, 0.0), axis=1, keepdims=True)
        return g, d

    no_edges = jnp.zeros((tile_r, 128), F32)

    r0 = rp_ref[...]
    pu0 = precond(r0)
    pl.semaphore_wait(barrier, ndev - 1)
    send_seg(0, pu0)
    load_rd.wait()

    def start(k, e):
        r = rd_ref[k]
        u = r * invd[...]
        us[0, k] = u
        gbuf[pl.ds(k, 1), :] = jnp.sum(r * u, axis=0, keepdims=True)
        return edges(0, k, u, e)

    send_edges(0, lax.fori_loop(0, batch, start, no_edges))
    send_cont(0)
    load_mat.wait()
    high = mat_ref[...].astype(jnp.bfloat16)
    mh[...] = high
    ml[...] = (mat_ref[...] - high.astype(F32)).astype(jnp.bfloat16)

    package_product(0)
    ct0 = wait_halos(0)

    def first_image(k, e):
        u = us[0, k]
        m = image(0, k, u, ct0)
        ms[0, k] = m
        dbuf[pl.ds(k, 1), :] = jnp.sum(diag[...] * (m * u), axis=0, keepdims=True)
        return edges(1, k, m, e)

    e1 = lax.fori_loop(0, batch, first_image, no_edges)
    pw0 = package_image(0, pu0)
    pm0 = precond(pw0)
    send_seg(1, pm0)
    send_edges(1, e1)
    send_sums(0, total(gbuf, r0, pu0), total(dbuf, pw0, pu0))
    send_cont(1)

    package_product(1)
    ct1 = wait_halos(1)

    def second_image(k, c):
        ks[0, k] = image(1, k, ms[0, k], ct1)
        return c

    lax.fori_loop(0, batch, second_image, 0)
    pn0 = package_image(1, pm0)
    g0, d0 = take_sums(0)
    alpha0 = g0 / d0
    put(0, alpha0)
    pu1 = pu0 - alpha0 * pm0
    pw1 = pw0 - alpha0 * pn0
    r1 = r0 - alpha0 * pw0
    pm1 = precond(pw1)
    send_seg(2, pm1)

    def second_step(k, e):
        one = pl.ds(k, 1)
        a = cf[0, one, :]
        u = us[0, k] - a * ms[0, k]
        m = ms[0, k] - a * ks[0, k]
        us[1, k] = u
        ms[1, k] = m
        du = diag[...] * u
        gbuf[one, :] = jnp.sum(du * u, axis=0, keepdims=True)
        dbuf[one, :] = jnp.sum(du * m, axis=0, keepdims=True)
        return edges(2, k, m, e)

    e2 = lax.fori_loop(0, batch, second_step, no_edges)
    send_edges(2, e2)
    send_sums(1, total(gbuf, r1, pu1), total(dbuf, pw1, pu1))
    send_cont(2)

    package_product(2)
    ct2 = wait_halos(2)
    g1, d1 = take_sums(1)
    beta1 = g1 / g0
    alpha1 = g1 / (d1 - beta1 * g1 / alpha0)
    put(1, alpha1)
    put(2, beta1)

    def last_step(k, c):
        one = pl.ds(k, 1)
        a = cf[1, one, :]
        b = cf[2, one, :]
        m1 = ms[1, k]
        n = image(2, k, m1, ct2) + b * ks[0, k]
        u = us[1, k] - a * (m1 + b * ms[0, k])
        m = m1 - a * n
        us[2, k] = u
        du = diag[...] * u
        gbuf[one, :] = jnp.sum(du * u, axis=0, keepdims=True)
        dbuf[one, :] = jnp.sum(du * m, axis=0, keepdims=True)
        return c

    lax.fori_loop(0, batch, last_step, 0)
    pn1 = package_image(2, pm1)
    pu2 = pu1 - alpha1 * (pm1 + beta1 * pm0)
    pw2 = pw1 - alpha1 * (pn1 + beta1 * pn0)
    r2 = r1 - alpha1 * (pw1 + beta1 * pw0)
    send_sums(2, total(gbuf, r2, pu2), total(dbuf, pw2, pu2))

    mine = me // nrows == icol
    for it in range(ITERS):
        drain(seg.at[it, 0 : ncols - 1], ssend.at[it])
        drain(cont.at[it, 0 : ncols - 1], csendm.at[it])

        @pl.when(mine)
        def _():
            drain(part.at[it, 0 : nrows - 1], psend.at[it])

        @pl.when(jnp.logical_not(mine))
        def _():
            drain(part.at[it], psend.at[it])

        for side, copy in enumerate(halos(it)):
            pl.when(has[side])(copy.wait_send)

    g2, d2 = take_sums(2)
    beta2 = g2 / g1
    c2 = g2 / (d2 - beta2 * g2 / alpha1)
    c1 = alpha1 + c2 * beta2
    c0 = alpha0 + c1 * beta1
    put(0, c0)
    put(1, c1)
    put(2, c2)
    xp_ref[...] = c0 * pu0 + c1 * pu1 + c2 * pu2

    def finish(k, c):
        one = pl.ds(k, 1)
        xd_ref[k] = cf[0, one, :] * us[0, k] + cf[1, one, :] * us[1, k] + cf[2, one, :] * us[2, k]
        return c

    lax.fori_loop(0, batch, finish, 0)
    for it in range(ITERS):
        drain(red.at[it, 0 : ndev - 1], rsendm.at[it])


def solution(mesh):
    nrows, ncols = mesh.shape["row"], mesh.shape["col"]

    def body(die_current, die_shunt, pkg_current, pkg_matrix, pkg_block_inv, bump_node, bump_conductance):
        batch, tile_r, tile_c = die_current.shape
        local_n = pkg_current.shape[1]
        bumps = bump_node.shape[0]
        lat_rows = bumps // BUMP_C // nrows
        lat_cols = BUMP_C // ncols
        nodes = bump_node.reshape(-1, 128)
        cond = bump_conductance.reshape(-1, 128)
        noff = len(pairs_by_offset(lat_rows, ncols, local_n))
        ndev = nrows * ncols
        vm = pltpu.VMEM
        dma = pltpu.SemaphoreType.DMA
        row = (batch, tile_c)
        return pl.pallas_call(
            functools.partial(kernel, nrows, ncols, lat_rows, lat_cols),
            out_shape=(
                jax.ShapeDtypeStruct(die_current.shape, F32),
                jax.ShapeDtypeStruct(pkg_current.shape, F32),
            ),
            in_specs=[
                pl.BlockSpec(memory_space=pltpu.HBM if i in (0, 3) else pltpu.VMEM)
                for i in range(7)
            ],
            out_specs=(pl.BlockSpec(memory_space=pltpu.VMEM),) * 2,
            scratch_shapes=[
                vm(die_current.shape, F32),
                vm(pkg_matrix.shape, F32),
                vm((3,) + die_current.shape, F32),
                vm((2,) + die_current.shape, F32),
                vm((1,) + die_current.shape, F32),
                vm((tile_r, tile_c), F32),
                vm((tile_r, tile_c), F32),
                vm((tile_r, tile_c), F32),
                vm((tile_r, tile_c), F32),
                vm(pkg_matrix.shape, jnp.bfloat16),
                vm(pkg_matrix.shape, jnp.bfloat16),
                vm((local_n, local_n), F32),
                vm(row, F32),
                vm(row, F32),
                vm((3,) + row, F32),
                vm((lat_rows,) + row, F32),
                vm((lat_rows,) + row, F32),
                vm((noff, tile_c, local_n), jnp.bfloat16),
                vm((noff, local_n, tile_c), jnp.bfloat16),
                vm((ITERS, 2) + row, F32),
                vm((ITERS, 2) + row, F32),
                vm((ITERS, 2, batch, tile_r), F32),
                vm((ITERS, 2, batch, tile_r), F32),
                vm((ITERS, ncols, batch, local_n), F32),
                vm((ITERS, nrows, batch, local_n), F32),
                vm((ITERS, nrows, batch, local_n), F32),
                vm((ITERS, ncols, batch, local_n), F32),
                vm((ITERS, ncols, batch, local_n), F32),
                vm((ITERS, ndev, 1, 128), F32),
                dma((ITERS, 4)),
                dma((ITERS, 4)),
                dma((ITERS,)),
                dma((ITERS,)),
                dma((ITERS,)),
                dma((ITERS,)),
                dma((ITERS,)),
                dma((ITERS,)),
                dma((ITERS,)),
                dma((ITERS,)),
                dma((2,)),
            ],
            compiler_params=pltpu.CompilerParams(
                collective_id=0, has_side_effects=True, vmem_limit_bytes=48 << 20
            ),
        )(die_current, die_shunt, pkg_current, pkg_matrix, pkg_block_inv, nodes, cond)

    placed = (
        P(None, "row", "col"),
        P("row", "col"),
        P(None, ("row", "col")),
        P("row", "col"),
        P(("row", "col"), None, None),
        P(),
        P(),
    )
    return jax.shard_map(
        body,
        mesh=mesh,
        in_specs=placed,
        out_specs=(P(None, "row", "col"), P(None, ("row", "col"))),
        check_vma=False,
    )
```

```python
import functools

import jax
import jax.numpy as jnp
from jax import lax
from jax.experimental import pallas as pl
from jax.experimental.pallas import tpu as pltpu
from jax.sharding import PartitionSpec as P

BUMP_C = 64
PB = 32
ITERS = 3
MESH = pl.DeviceIdType.MESH
HI = lax.Precision.HIGHEST
F32 = jnp.float32


def drain(ref, sem):
    pltpu.make_async_copy(ref, ref, sem).wait()


def split3(v):
    high = v.astype(jnp.bfloat16)
    rest = v - high.astype(F32)
    mid = rest.astype(jnp.bfloat16)
    return [high, mid, (rest - mid.astype(F32)).astype(jnp.bfloat16)]


def exact_pick(parts, onehot):
    rows = sum(p.shape[0] for p in parts)
    stacked = jnp.concatenate(parts, axis=0) if len(parts) > 1 else parts[0]
    out = jnp.dot(
        jnp.concatenate(split3(stacked), axis=0), onehot, preferred_element_type=F32
    )
    return out[:rows] + out[rows : 2 * rows] + out[2 * rows :]


def pairs_by_offset(lat_rows, ncols, local_n):
    groups = {}
    for lr in range(lat_rows):
        for j in range(ncols):
            if lr * BUMP_C < (j + 1) * local_n and j * local_n < (lr + 1) * BUMP_C:
                groups.setdefault(lr * BUMP_C - j * local_n, []).append((lr, j))
    return sorted(groups.items())


def kernel(
    nrows, ncols, lat_rows, lat_cols,
    rd_hbm, shunt_hbm, rp_hbm, mat_hbm, inv_hbm, node_hbm, cond_hbm,
    xd_hbm, xp_hbm,
    rd_ref, mat_ref, shunt_ref, rp_ref, inv_ref, node_ref, cond_ref, xp_ref, us, ms, ks, diag, invd, mask, cinv, mh, ml, bd, gbuf, dbuf, cf, abuf, vpx,
    emb, embt, rsend, hr, csend, hc, seg, part, rec, cont, dat, red,
    hsend, hrecv, ssend, srecv, psend, precv, csendm, drecv, rsendm, rrecv, loadsem, outsem,
):
    ndev = nrows * ncols
    irow = lax.axis_index("row")
    icol = lax.axis_index("col")
    me = irow * ncols + icol
    batch, tile_r, tile_c = rd_ref.shape
    local_n = rp_ref.shape[1]
    cell_r = tile_r // lat_rows
    cell_c = tile_c // lat_cols
    total_c = tile_c * ncols
    groups = pairs_by_offset(lat_rows, ncols, local_n)

    loads = [
        pltpu.make_async_copy(src, dst, loadsem.at[i])
        for i, (src, dst) in enumerate(
            (
                (node_hbm, node_ref),
                (cond_hbm, cond_ref),
                (shunt_hbm, shunt_ref),
                (inv_hbm, inv_ref),
                (rp_hbm, rp_ref),
                (rd_hbm, rd_ref),
                (mat_hbm, mat_ref),
            )
        )
    ]
    for load in loads:
        load.start()

    hr[...] = jnp.zeros_like(hr)
    hc[...] = jnp.zeros_like(hc)
    barrier = pltpu.get_barrier_semaphore()

    def greet(d, c):
        t = lax.rem(me + d, ndev)
        pl.semaphore_signal(
            barrier, inc=1, device_id=(t // ncols, lax.rem(t, ncols)), device_id_type=MESH
        )
        return c

    lax.fori_loop(1, ndev, greet, 0)

    node_c = icol * lat_cols + lax.broadcasted_iota(jnp.int32, (tile_c, local_n), 0) // cell_c
    node_l = lax.broadcasted_iota(jnp.int32, (tile_c, local_n), 1)
    node_ct = icol * lat_cols + lax.broadcasted_iota(jnp.int32, (local_n, tile_c), 1) // cell_c
    node_lt = lax.broadcasted_iota(jnp.int32, (local_n, tile_c), 0)
    for g, (off, members) in enumerate(groups):
        emb[g] = jnp.where(node_c + off == node_l, 1.0, 0.0).astype(jnp.bfloat16)
        embt[g] = jnp.where(node_ct + off == node_lt, 1.0, 0.0).astype(jnp.bfloat16)
    bd[...] = jnp.zeros_like(bd)

    for load in loads[:5]:
        load.wait()
    seg_rows = lat_rows * BUMP_C // 128
    per_row = 128 // BUMP_C
    nodes = node_ref[pl.ds(irow * seg_rows, seg_rows), :]
    conds = cond_ref[pl.ds(irow * seg_rows, seg_rows), :]
    node_r = lax.rem(nodes // total_c, cell_r).astype(F32)
    node_q = lax.rem(lax.rem(nodes, total_c), cell_c).astype(F32)
    tall = jnp.concatenate([node_r, node_q, conds], axis=0)
    tall = jnp.concatenate([tall, jnp.zeros((-tall.shape[0] % 8, 128), F32)], axis=0)
    wide_l = lax.broadcasted_iota(jnp.int32, (128, tile_c), 0)
    wide_c = lax.broadcasted_iota(jnp.int32, (128, tile_c), 1) // cell_c + icol * lat_cols
    row_c = lax.broadcasted_iota(jnp.int32, (cell_r, tile_c), 0).astype(F32)
    lane_c = lax.rem(lax.broadcasted_iota(jnp.int32, (cell_r, tile_c), 1), cell_c).astype(F32)
    for q in range(per_row):
        pick = jnp.where(wide_l == wide_c + q * BUMP_C, 1.0, 0.0).astype(jnp.bfloat16)
        flat = exact_pick([tall], pick)
        for i in range(seg_rows):
            lr = i * per_row + q
            rs = slice(lr * cell_r, (lr + 1) * cell_r)
            hit = (row_c == flat[i : i + 1, :]) & (
                lane_c == flat[seg_rows + i : seg_rows + i + 1, :]
            )
            m = jnp.where(hit, 1.0, 0.0)
            cm = m * flat[2 * seg_rows + i : 2 * seg_rows + i + 1, :]
            dg = 4.0 + shunt_ref[rs, :] + cm
            iv = 1.0 / dg
            mask[rs, :] = m
            diag[rs, :] = dg
            invd[rs, :] = iv
            cinv[rs, :] = cm * iv
    first = me * local_n
    mine_l = lax.broadcasted_iota(jnp.int32, (128, local_n), 0)
    mine_n = lax.broadcasted_iota(jnp.int32, (128, local_n), 1) + lax.rem(first, 128)
    own = jnp.broadcast_to(cond_ref[pl.ds(first // 128, 1), :], (8, 128))
    chere = exact_pick([own], jnp.where(mine_l == mine_n, 1.0, 0.0).astype(jnp.bfloat16))[0:1]

    for q in range(local_n // PB):
        bd[q * PB : (q + 1) * PB, q * PB : (q + 1) * PB] = inv_ref[q]

    lane_e = lax.broadcasted_iota(jnp.int32, (tile_r, 128), 1)
    row_i = lax.broadcasted_iota(jnp.int32, (tile_r, tile_c), 0)
    lane_i = lax.broadcasted_iota(jnp.int32, (tile_r, tile_c), 1)
    sub_k = lax.broadcasted_iota(jnp.int32, (batch, 128), 0)
    lane_k = lax.broadcasted_iota(jnp.int32, (batch, 128), 1)

    def remote(src, dst, ssem, rsem, r, c):
        return pltpu.make_async_remote_copy(
            src_ref=src, dst_ref=dst, send_sem=ssem, recv_sem=rsem,
            device_id=(r, c), device_id_type=MESH,
        )

    has = (irow > 0, irow < nrows - 1, icol > 0, icol < ncols - 1)

    def halos(it):
        return (
            remote(rsend.at[it, 0], hr.at[it, 1], hsend.at[it, 0], hrecv.at[it, 1], irow - 1, icol),
            remote(rsend.at[it, 1], hr.at[it, 0], hsend.at[it, 1], hrecv.at[it, 0], irow + 1, icol),
            remote(csend.at[it, 0], hc.at[it, 1], hsend.at[it, 2], hrecv.at[it, 3], irow, icol - 1),
            remote(csend.at[it, 1], hc.at[it, 0], hsend.at[it, 3], hrecv.at[it, 2], irow, icol + 1),
        )

    def put(slot, value):
        cf[slot] = jnp.broadcast_to(value, (batch, tile_c))

    def precond(v):
        return lax.dot_general(v, bd[...], (((1,), (1,)), ((), ())), precision=HI)

    def send_seg(it, v):
        seg[it, icol] = v
        for d in range(1, ncols):
            remote(
                seg.at[it, icol], seg.at[it, icol], ssend.at[it], srecv.at[it],
                irow, lax.rem(icol + d, ncols),
            ).start()

    def edges(it, k, v, e):
        one = pl.ds(k, 1)
        rsend[it, 0, one, :] = v[0:1, :]
        rsend[it, 1, one, :] = v[tile_r - 1 : tile_r, :]
        mv = v * mask[...]
        for lr in range(lat_rows):
            abuf[lr, one, :] = jnp.sum(mv[lr * cell_r : (lr + 1) * cell_r], axis=0, keepdims=True)
        e = jnp.where(lane_e == k, v[:, 0:1], e)
        return jnp.where(lane_e == k + batch, v[:, tile_c - 1 : tile_c], e)

    def send_edges(it, e):
        et = e.T
        csend[it, 0] = et[0:batch, :]
        csend[it, 1] = et[batch : 2 * batch, :]
        for side, copy in enumerate(halos(it)):
            pl.when(has[side])(copy.start)

    def send_cont(it):
        totals = [None] * ncols
        for g, (off, members) in enumerate(groups):
            out = exact_pick([abuf[lr] for lr, j in members], emb[g])
            for i, (lr, j) in enumerate(members):
                term = out[i * batch : (i + 1) * batch]
                totals[j] = term if totals[j] is None else totals[j] + term
        for j in range(ncols):
            cont[it, j] = totals[j]
        dat[it, icol] = cont[it, icol]
        for d in range(1, ncols):
            t = lax.rem(icol + d, ncols)
            remote(
                cont.at[it, t], dat.at[it, icol], csendm.at[it], drecv.at[it], irow, t
            ).start()

    def package_product(it):
        drain(seg.at[it, 0 : ncols - 1], srecv.at[it])
        acc = None
        for j in range(ncols):
            v = seg[it, j]
            vh = v.astype(jnp.bfloat16)
            vl = (v - vh.astype(F32)).astype(jnp.bfloat16)
            span = slice(j * local_n, (j + 1) * local_n)
            both = jnp.dot(
                jnp.concatenate([vh, vl], axis=0), mh[span, :], preferred_element_type=F32
            )
            term = both[:batch] + both[batch:]
            term += jnp.dot(vh, ml[span, :], preferred_element_type=F32)
            acc = term if acc is None else acc + term
        for m in range(nrows):
            part[it, m] = acc[:, m * local_n : (m + 1) * local_n]
        for m in range(nrows):
            n = icol * nrows + m
            copy = remote(
                part.at[it, m], rec.at[it, irow], psend.at[it], precv.at[it],
                n // ncols, lax.rem(n, ncols),
            )
            pl.when(n != me)(copy.start)

            @pl.when(n == me)
            def _():
                pltpu.make_async_copy(part.at[it, m], rec.at[it, irow], precv.at[it]).start()

        totals = [None] * lat_rows
        for g, (off, members) in enumerate(groups):
            out = exact_pick([seg[it, j] for lr, j in members], embt[g])
            for i, (lr, j) in enumerate(members):
                term = out[i * batch : (i + 1) * batch]
                totals[lr] = term if totals[lr] is None else totals[lr] + term
        for lr in range(lat_rows):
            vpx[lr] = totals[lr]

    def wait_halos(it):
        for side, index in enumerate(((hr, 0), (hr, 1), (hc, 0), (hc, 1))):
            ref, pos = index

            @pl.when(has[side])
            def _():
                drain(ref.at[it, pos], hrecv.at[it, side])

        return jnp.concatenate(
            [hc[it, 0], hc[it, 1], jnp.zeros((128 - 2 * batch, tile_r), F32)], axis=0
        ).T

    def image(it, k, v, ct):
        one = pl.ds(k, 1)
        left = jnp.sum(jnp.where(lane_e == k, ct, 0.0), axis=1, keepdims=True)
        right = jnp.sum(jnp.where(lane_e == k + batch, ct, 0.0), axis=1, keepdims=True)
        near = jnp.where(row_i == 0, hr[it, 0, one, :], pltpu.roll(v, 1, 0))
        near += jnp.where(row_i == tile_r - 1, hr[it, 1, one, :], pltpu.roll(v, tile_r - 1, 0))
        near += jnp.where(lane_i == 0, left, pltpu.roll(v, 1, 1))
        near += jnp.where(lane_i == tile_c - 1, right, pltpu.roll(v, tile_c - 1, 1))
        feed = jnp.concatenate(
            [
                cinv[lr * cell_r : (lr + 1) * cell_r, :] * vpx[lr, one, :]
                for lr in range(lat_rows)
            ],
            axis=0,
        )
        return v - near * invd[...] - feed

    def package_image(it, v):
        drain(rec.at[it], precv.at[it])
        drain(dat.at[it, 0 : ncols - 1], drecv.at[it])
        out = rec[it, 0]
        for i in range(1, nrows):
            out += rec[it, i]
        die_at = dat[it, 0]
        for j in range(1, ncols):
            die_at += dat[it, j]
        return out + chere * (v - die_at)

    def total(buf, a, b):
        return jnp.sum(buf[...], axis=1, keepdims=True) + jnp.sum(a * b, axis=1, keepdims=True)

    def send_sums(it, g, d):
        line = jnp.where(lane_k == sub_k, g, 0.0) + jnp.where(lane_k == sub_k + batch, d, 0.0)
        red[it, me] = jnp.sum(line, axis=0, keepdims=True)

        def spread(d, c):
            t = lax.rem(me + d, ndev)
            remote(
                red.at[it, me], red.at[it, me], rsendm.at[it], rrecv.at[it],
                t // ncols, lax.rem(t, ncols),
            ).start()
            return c

        lax.fori_loop(1, ndev, spread, 0)

    def take_sums(it):
        drain(red.at[it, 0 : ndev - 1], rrecv.at[it])
        line = jnp.sum(red[it], axis=0)
        g = jnp.sum(jnp.where(lane_k == sub_k, line, 0.0), axis=1, keepdims=True)
        d = jnp.sum(jnp.where(lane_k == sub_k + batch, line, 0.0), axis=1, keepdims=True)
        return g, d

    no_edges = jnp.zeros((tile_r, 128), F32)

    r0 = rp_ref[...]
    pu0 = precond(r0)
    pl.semaphore_wait(barrier, ndev - 1)
    send_seg(0, pu0)
    loads[5].wait()

    def start(k, e):
        r = rd_ref[k]
        u = r * invd[...]
        us[0, k] = u
        gbuf[pl.ds(k, 1), :] = jnp.sum(r * u, axis=0, keepdims=True)
        return edges(0, k, u, e)

    send_edges(0, lax.fori_loop(0, batch, start, no_edges))
    send_cont(0)
    loads[6].wait()
    high = mat_ref[...].astype(jnp.bfloat16)
    mh[...] = high
    ml[...] = (mat_ref[...] - high.astype(F32)).astype(jnp.bfloat16)

    package_product(0)
    ct0 = wait_halos(0)

    def first_image(k, e):
        u = us[0, k]
        m = image(0, k, u, ct0)
        ms[0, k] = m
        dbuf[pl.ds(k, 1), :] = jnp.sum(diag[...] * (m * u), axis=0, keepdims=True)
        return edges(1, k, m, e)

    e1 = lax.fori_loop(0, batch, first_image, no_edges)
    pw0 = package_image(0, pu0)
    pm0 = precond(pw0)
    send_seg(1, pm0)
    send_edges(1, e1)
    send_sums(0, total(gbuf, r0, pu0), total(dbuf, pw0, pu0))
    send_cont(1)

    package_product(1)
    ct1 = wait_halos(1)

    def second_image(k, c):
        ks[0, k] = image(1, k, ms[0, k], ct1)
        return c

    lax.fori_loop(0, batch, second_image, 0)
    pn0 = package_image(1, pm0)
    g0, d0 = take_sums(0)
    alpha0 = g0 / d0
    put(0, alpha0)
    pu1 = pu0 - alpha0 * pm0
    pw1 = pw0 - alpha0 * pn0
    r1 = r0 - alpha0 * pw0
    pm1 = precond(pw1)
    send_seg(2, pm1)

    def second_step(k, e):
        one = pl.ds(k, 1)
        a = cf[0, one, :]
        u = us[0, k] - a * ms[0, k]
        m = ms[0, k] - a * ks[0, k]
        us[1, k] = u
        ms[1, k] = m
        du = diag[...] * u
        gbuf[one, :] = jnp.sum(du * u, axis=0, keepdims=True)
        dbuf[one, :] = jnp.sum(du * m, axis=0, keepdims=True)
        return edges(2, k, m, e)

    e2 = lax.fori_loop(0, batch, second_step, no_edges)
    send_edges(2, e2)
    send_sums(1, total(gbuf, r1, pu1), total(dbuf, pw1, pu1))
    send_cont(2)

    package_product(2)
    ct2 = wait_halos(2)

    def third_image(k, c):
        ks[1, k] = image(2, k, ms[1, k], ct2)
        return c

    lax.fori_loop(0, batch, third_image, 0)
    g1, d1 = take_sums(1)
    beta1 = g1 / g0
    alpha1 = g1 / (d1 - beta1 * g1 / alpha0)
    put(1, alpha1)
    put(2, beta1)

    def last_step(k, c):
        one = pl.ds(k, 1)
        a = cf[1, one, :]
        b = cf[2, one, :]
        m1 = ms[1, k]
        u = us[1, k] - a * (m1 + b * ms[0, k])
        m = m1 - a * (ks[1, k] + b * ks[0, k])
        us[2, k] = u
        du = diag[...] * u
        gbuf[one, :] = jnp.sum(du * u, axis=0, keepdims=True)
        dbuf[one, :] = jnp.sum(du * m, axis=0, keepdims=True)
        return c

    lax.fori_loop(0, batch, last_step, 0)
    pn1 = package_image(2, pm1)
    pu2 = pu1 - alpha1 * (pm1 + beta1 * pm0)
    pw2 = pw1 - alpha1 * (pn1 + beta1 * pn0)
    r2 = r1 - alpha1 * (pw1 + beta1 * pw0)
    send_sums(2, total(gbuf, r2, pu2), total(dbuf, pw2, pu2))

    mine = me // nrows == icol
    for it in range(ITERS):
        drain(seg.at[it, 0 : ncols - 1], ssend.at[it])
        drain(cont.at[it, 0 : ncols - 1], csendm.at[it])

        @pl.when(mine)
        def _():
            drain(part.at[it, 0 : nrows - 1], psend.at[it])

        @pl.when(jnp.logical_not(mine))
        def _():
            drain(part.at[it], psend.at[it])

        for side, copy in enumerate(halos(it)):
            pl.when(has[side])(copy.wait_send)

    g2, d2 = take_sums(2)
    beta2 = g2 / g1
    c2 = g2 / (d2 - beta2 * g2 / alpha1)
    c1 = alpha1 + c2 * beta2
    c0 = alpha0 + c1 * beta1
    put(0, c0)
    put(1, c1)
    put(2, c2)
    xp_ref[...] = c0 * pu0 + c1 * pu1 + c2 * pu2
    xp_out = pltpu.make_async_copy(xp_ref, xp_hbm, outsem.at[0])
    xp_out.start()

    def finish(k, c):
        one = pl.ds(k, 1)
        rd_ref[k] = cf[0, one, :] * us[0, k] + cf[1, one, :] * us[1, k] + cf[2, one, :] * us[2, k]
        pltpu.make_async_copy(rd_ref.at[k], xd_hbm.at[k], outsem.at[1]).start()
        return c

    lax.fori_loop(0, batch, finish, 0)
    xp_out.wait()
    pltpu.make_async_copy(rd_ref, xd_hbm, outsem.at[1]).wait()
    for it in range(ITERS):
        drain(red.at[it, 0 : ndev - 1], rsendm.at[it])


def solution(mesh):
    nrows, ncols = mesh.shape["row"], mesh.shape["col"]

    def body(die_current, die_shunt, pkg_current, pkg_matrix, pkg_block_inv, bump_node, bump_conductance):
        batch, tile_r, tile_c = die_current.shape
        local_n = pkg_current.shape[1]
        bumps = bump_node.shape[0]
        lat_rows = bumps // BUMP_C // nrows
        lat_cols = BUMP_C // ncols
        nodes = bump_node.reshape(-1, 128)
        cond = bump_conductance.reshape(-1, 128)
        noff = len(pairs_by_offset(lat_rows, ncols, local_n))
        ndev = nrows * ncols
        vm = pltpu.VMEM
        dma = pltpu.SemaphoreType.DMA
        row = (batch, tile_c)
        return pl.pallas_call(
            functools.partial(kernel, nrows, ncols, lat_rows, lat_cols),
            out_shape=(
                jax.ShapeDtypeStruct(die_current.shape, F32),
                jax.ShapeDtypeStruct(pkg_current.shape, F32),
            ),
            in_specs=[pl.BlockSpec(memory_space=pltpu.HBM)] * 7,
            out_specs=(pl.BlockSpec(memory_space=pltpu.HBM),) * 2,
            scratch_shapes=[
                vm(die_current.shape, F32),
                vm(pkg_matrix.shape, F32),
                vm(die_shunt.shape, F32),
                vm(pkg_current.shape, F32),
                vm(pkg_block_inv.shape, F32),
                vm(nodes.shape, jnp.int32),
                vm(cond.shape, F32),
                vm(pkg_current.shape, F32),
                vm((3,) + die_current.shape, F32),
                vm((2,) + die_current.shape, F32),
                vm((2,) + die_current.shape, F32),
                vm((tile_r, tile_c), F32),
                vm((tile_r, tile_c), F32),
                vm((tile_r, tile_c), F32),
                vm((tile_r, tile_c), F32),
                vm(pkg_matrix.shape, jnp.bfloat16),
                vm(pkg_matrix.shape, jnp.bfloat16),
                vm((local_n, local_n), F32),
                vm(row, F32),
                vm(row, F32),
                vm((3,) + row, F32),
                vm((lat_rows,) + row, F32),
                vm((lat_rows,) + row, F32),
                vm((noff, tile_c, local_n), jnp.bfloat16),
                vm((noff, local_n, tile_c), jnp.bfloat16),
                vm((ITERS, 2) + row, F32),
                vm((ITERS, 2) + row, F32),
                vm((ITERS, 2, batch, tile_r), F32),
                vm((ITERS, 2, batch, tile_r), F32),
                vm((ITERS, ncols, batch, local_n), F32),
                vm((ITERS, nrows, batch, local_n), F32),
                vm((ITERS, nrows, batch, local_n), F32),
                vm((ITERS, ncols, batch, local_n), F32),
                vm((ITERS, ncols, batch, local_n), F32),
                vm((ITERS, ndev, 1, 128), F32),
                dma((ITERS, 4)),
                dma((ITERS, 4)),
                dma((ITERS,)),
                dma((ITERS,)),
                dma((ITERS,)),
                dma((ITERS,)),
                dma((ITERS,)),
                dma((ITERS,)),
                dma((ITERS,)),
                dma((ITERS,)),
                dma((7,)),
                dma((2,)),
            ],
            compiler_params=pltpu.CompilerParams(
                collective_id=0, has_side_effects=True, vmem_limit_bytes=67043328
            ),
        )(die_current, die_shunt, pkg_current, pkg_matrix, pkg_block_inv, nodes, cond)

    placed = (
        P(None, "row", "col"),
        P("row", "col"),
        P(None, ("row", "col")),
        P("row", "col"),
        P(("row", "col"), None, None),
        P(),
        P(),
    )
    return jax.shard_map(
        body,
        mesh=mesh,
        in_specs=placed,
        out_specs=(P(None, "row", "col"), P(None, ("row", "col"))),
        check_vma=False,
    )
```

```python
import functools

import jax
import jax.numpy as jnp
from jax import lax
from jax.experimental import pallas as pl
from jax.experimental.pallas import tpu as pltpu
from jax.sharding import PartitionSpec as P

BUMP_C = 64
PB = 32
ITERS = 3
MESH = pl.DeviceIdType.MESH
HI = lax.Precision.HIGHEST
F32 = jnp.float32


def drain(ref, sem):
    pltpu.make_async_copy(ref, ref, sem).wait()


def split3(v):
    high = v.astype(jnp.bfloat16)
    rest = v - high.astype(F32)
    mid = rest.astype(jnp.bfloat16)
    return [high, mid, (rest - mid.astype(F32)).astype(jnp.bfloat16)]


def exact_pick(parts, onehot):
    rows = sum(p.shape[0] for p in parts)
    stacked = jnp.concatenate(parts, axis=0) if len(parts) > 1 else parts[0]
    out = jnp.dot(
        jnp.concatenate(split3(stacked), axis=0), onehot, preferred_element_type=F32
    )
    return out[:rows] + out[rows : 2 * rows] + out[2 * rows :]


def pairs_by_offset(lat_rows, ncols, local_n):
    groups = {}
    for lr in range(lat_rows):
        for j in range(ncols):
            if lr * BUMP_C < (j + 1) * local_n and j * local_n < (lr + 1) * BUMP_C:
                groups.setdefault(lr * BUMP_C - j * local_n, []).append((lr, j))
    return sorted(groups.items())


def kernel(
    nrows, ncols, lat_rows, lat_cols,
    rd_hbm, shunt_hbm, rp_hbm, mat_hbm, inv_hbm, node_hbm, cond_hbm,
    us_hbm, cf_hbm, xp_hbm,
    rd_ref, mat_ref, shunt_ref, rp_ref, inv_ref, node_ref, cond_ref, xp_ref, us, ms, ks, diag, invd, mask, cinv, mh, ml, bd, gbuf, dbuf, cf, abuf, vpx,
    emb, embt, rsend, hr, csend, hc, seg, part, rec, cont, dat, red,
    hsend, hrecv, ssend, srecv, psend, precv, csendm, drecv, rsendm, rrecv, loadsem, outsem,
):
    ndev = nrows * ncols
    irow = lax.axis_index("row")
    icol = lax.axis_index("col")
    me = irow * ncols + icol
    batch, tile_r, tile_c = rd_ref.shape
    local_n = rp_ref.shape[1]
    cell_r = tile_r // lat_rows
    cell_c = tile_c // lat_cols
    total_c = tile_c * ncols
    groups = pairs_by_offset(lat_rows, ncols, local_n)

    loads = [
        pltpu.make_async_copy(src, dst, loadsem.at[i])
        for i, (src, dst) in enumerate(
            (
                (node_hbm, node_ref),
                (cond_hbm, cond_ref),
                (shunt_hbm, shunt_ref),
                (inv_hbm, inv_ref),
                (rp_hbm, rp_ref),
                (rd_hbm, rd_ref),
                (mat_hbm, mat_ref),
            )
        )
    ]
    for load in loads:
        load.start()

    hr[...] = jnp.zeros_like(hr)
    hc[...] = jnp.zeros_like(hc)
    barrier = pltpu.get_barrier_semaphore()

    def greet(d, c):
        t = lax.rem(me + d, ndev)
        pl.semaphore_signal(
            barrier, inc=1, device_id=(t // ncols, lax.rem(t, ncols)), device_id_type=MESH
        )
        return c

    lax.fori_loop(1, ndev, greet, 0)

    node_c = icol * lat_cols + lax.broadcasted_iota(jnp.int32, (tile_c, local_n), 0) // cell_c
    node_l = lax.broadcasted_iota(jnp.int32, (tile_c, local_n), 1)
    node_ct = icol * lat_cols + lax.broadcasted_iota(jnp.int32, (local_n, tile_c), 1) // cell_c
    node_lt = lax.broadcasted_iota(jnp.int32, (local_n, tile_c), 0)
    for g, (off, members) in enumerate(groups):
        emb[g] = jnp.where(node_c + off == node_l, 1.0, 0.0).astype(jnp.bfloat16)
        embt[g] = jnp.where(node_ct + off == node_lt, 1.0, 0.0).astype(jnp.bfloat16)
    bd[...] = jnp.zeros_like(bd)

    for load in loads[:5]:
        load.wait()
    seg_rows = lat_rows * BUMP_C // 128
    per_row = 128 // BUMP_C
    nodes = node_ref[pl.ds(irow * seg_rows, seg_rows), :]
    conds = cond_ref[pl.ds(irow * seg_rows, seg_rows), :]
    node_r = lax.rem(nodes // total_c, cell_r).astype(F32)
    node_q = lax.rem(lax.rem(nodes, total_c), cell_c).astype(F32)
    tall = jnp.concatenate([node_r, node_q, conds], axis=0)
    tall = jnp.concatenate([tall, jnp.zeros((-tall.shape[0] % 8, 128), F32)], axis=0)
    wide_l = lax.broadcasted_iota(jnp.int32, (128, tile_c), 0)
    wide_c = lax.broadcasted_iota(jnp.int32, (128, tile_c), 1) // cell_c + icol * lat_cols
    row_c = lax.broadcasted_iota(jnp.int32, (cell_r, tile_c), 0).astype(F32)
    lane_c = lax.rem(lax.broadcasted_iota(jnp.int32, (cell_r, tile_c), 1), cell_c).astype(F32)
    for q in range(per_row):
        pick = jnp.where(wide_l == wide_c + q * BUMP_C, 1.0, 0.0).astype(jnp.bfloat16)
        flat = exact_pick([tall], pick)
        for i in range(seg_rows):
            lr = i * per_row + q
            rs = slice(lr * cell_r, (lr + 1) * cell_r)
            hit = (row_c == flat[i : i + 1, :]) & (
                lane_c == flat[seg_rows + i : seg_rows + i + 1, :]
            )
            m = jnp.where(hit, 1.0, 0.0)
            cm = m * flat[2 * seg_rows + i : 2 * seg_rows + i + 1, :]
            dg = 4.0 + shunt_ref[rs, :] + cm
            iv = 1.0 / dg
            mask[rs, :] = m
            diag[rs, :] = dg
            invd[rs, :] = iv
            cinv[rs, :] = cm * iv
    first = me * local_n
    mine_l = lax.broadcasted_iota(jnp.int32, (128, local_n), 0)
    mine_n = lax.broadcasted_iota(jnp.int32, (128, local_n), 1) + lax.rem(first, 128)
    own = jnp.broadcast_to(cond_ref[pl.ds(first // 128, 1), :], (8, 128))
    chere = exact_pick([own], jnp.where(mine_l == mine_n, 1.0, 0.0).astype(jnp.bfloat16))[0:1]

    for q in range(local_n // PB):
        bd[q * PB : (q + 1) * PB, q * PB : (q + 1) * PB] = inv_ref[q]

    lane_e = lax.broadcasted_iota(jnp.int32, (tile_r, 128), 1)
    row_i = lax.broadcasted_iota(jnp.int32, (tile_r, tile_c), 0)
    lane_i = lax.broadcasted_iota(jnp.int32, (tile_r, tile_c), 1)
    sub_k = lax.broadcasted_iota(jnp.int32, (batch, 128), 0)
    lane_k = lax.broadcasted_iota(jnp.int32, (batch, 128), 1)

    def remote(src, dst, ssem, rsem, r, c):
        return pltpu.make_async_remote_copy(
            src_ref=src, dst_ref=dst, send_sem=ssem, recv_sem=rsem,
            device_id=(r, c), device_id_type=MESH,
        )

    has = (irow > 0, irow < nrows - 1, icol > 0, icol < ncols - 1)

    def halos(it):
        return (
            remote(rsend.at[it, 0], hr.at[it, 1], hsend.at[it, 0], hrecv.at[it, 1], irow - 1, icol),
            remote(rsend.at[it, 1], hr.at[it, 0], hsend.at[it, 1], hrecv.at[it, 0], irow + 1, icol),
            remote(csend.at[it, 0], hc.at[it, 1], hsend.at[it, 2], hrecv.at[it, 3], irow, icol - 1),
            remote(csend.at[it, 1], hc.at[it, 0], hsend.at[it, 3], hrecv.at[it, 2], irow, icol + 1),
        )

    def put(slot, value):
        cf[slot] = jnp.broadcast_to(value, (batch, tile_c))

    def precond(v):
        return lax.dot_general(v, bd[...], (((1,), (1,)), ((), ())), precision=HI)

    def send_seg(it, v):
        seg[it, icol] = v
        for d in range(1, ncols):
            remote(
                seg.at[it, icol], seg.at[it, icol], ssend.at[it], srecv.at[it],
                irow, lax.rem(icol + d, ncols),
            ).start()

    def edges(it, k, v, e):
        one = pl.ds(k, 1)
        rsend[it, 0, one, :] = v[0:1, :]
        rsend[it, 1, one, :] = v[tile_r - 1 : tile_r, :]
        mv = v * mask[...]
        for lr in range(lat_rows):
            abuf[lr, one, :] = jnp.sum(mv[lr * cell_r : (lr + 1) * cell_r], axis=0, keepdims=True)
        e = jnp.where(lane_e == k, v[:, 0:1], e)
        return jnp.where(lane_e == k + batch, v[:, tile_c - 1 : tile_c], e)

    def send_edges(it, e):
        et = e.T
        csend[it, 0] = et[0:batch, :]
        csend[it, 1] = et[batch : 2 * batch, :]
        for side, copy in enumerate(halos(it)):
            pl.when(has[side])(copy.start)

    def send_cont(it):
        totals = [None] * ncols
        for g, (off, members) in enumerate(groups):
            out = exact_pick([abuf[lr] for lr, j in members], emb[g])
            for i, (lr, j) in enumerate(members):
                term = out[i * batch : (i + 1) * batch]
                totals[j] = term if totals[j] is None else totals[j] + term
        for j in range(ncols):
            cont[it, j] = totals[j]
        dat[it, icol] = cont[it, icol]
        for d in range(1, ncols):
            t = lax.rem(icol + d, ncols)
            remote(
                cont.at[it, t], dat.at[it, icol], csendm.at[it], drecv.at[it], irow, t
            ).start()

    def package_product(it):
        drain(seg.at[it, 0 : ncols - 1], srecv.at[it])
        acc = None
        for j in range(ncols):
            v = seg[it, j]
            vh = v.astype(jnp.bfloat16)
            vl = (v - vh.astype(F32)).astype(jnp.bfloat16)
            span = slice(j * local_n, (j + 1) * local_n)
            both = jnp.dot(
                jnp.concatenate([vh, vl], axis=0), mh[span, :], preferred_element_type=F32
            )
            term = both[:batch] + both[batch:]
            term += jnp.dot(vh, ml[span, :], preferred_element_type=F32)
            acc = term if acc is None else acc + term
        for m in range(nrows):
            part[it, m] = acc[:, m * local_n : (m + 1) * local_n]
        for m in range(nrows):
            n = icol * nrows + m
            copy = remote(
                part.at[it, m], rec.at[it, irow], psend.at[it], precv.at[it],
                n // ncols, lax.rem(n, ncols),
            )
            pl.when(n != me)(copy.start)

            @pl.when(n == me)
            def _():
                pltpu.make_async_copy(part.at[it, m], rec.at[it, irow], precv.at[it]).start()

        totals = [None] * lat_rows
        for g, (off, members) in enumerate(groups):
            out = exact_pick([seg[it, j] for lr, j in members], embt[g])
            for i, (lr, j) in enumerate(members):
                term = out[i * batch : (i + 1) * batch]
                totals[lr] = term if totals[lr] is None else totals[lr] + term
        for lr in range(lat_rows):
            vpx[lr] = totals[lr]

    def wait_halos(it):
        for side, index in enumerate(((hr, 0), (hr, 1), (hc, 0), (hc, 1))):
            ref, pos = index

            @pl.when(has[side])
            def _():
                drain(ref.at[it, pos], hrecv.at[it, side])

        return jnp.concatenate(
            [hc[it, 0], hc[it, 1], jnp.zeros((128 - 2 * batch, tile_r), F32)], axis=0
        ).T

    def image(it, k, v, ct):
        one = pl.ds(k, 1)
        left = jnp.sum(jnp.where(lane_e == k, ct, 0.0), axis=1, keepdims=True)
        right = jnp.sum(jnp.where(lane_e == k + batch, ct, 0.0), axis=1, keepdims=True)
        near = jnp.where(row_i == 0, hr[it, 0, one, :], pltpu.roll(v, 1, 0))
        near += jnp.where(row_i == tile_r - 1, hr[it, 1, one, :], pltpu.roll(v, tile_r - 1, 0))
        near += jnp.where(lane_i == 0, left, pltpu.roll(v, 1, 1))
        near += jnp.where(lane_i == tile_c - 1, right, pltpu.roll(v, tile_c - 1, 1))
        feed = jnp.concatenate(
            [
                cinv[lr * cell_r : (lr + 1) * cell_r, :] * vpx[lr, one, :]
                for lr in range(lat_rows)
            ],
            axis=0,
        )
        return v - near * invd[...] - feed

    def package_image(it, v):
        drain(rec.at[it], precv.at[it])
        drain(dat.at[it, 0 : ncols - 1], drecv.at[it])
        out = rec[it, 0]
        for i in range(1, nrows):
            out += rec[it, i]
        die_at = dat[it, 0]
        for j in range(1, ncols):
            die_at += dat[it, j]
        return out + chere * (v - die_at)

    def total(buf, a, b):
        return jnp.sum(buf[...], axis=1, keepdims=True) + jnp.sum(a * b, axis=1, keepdims=True)

    def send_sums(it, g, d):
        line = jnp.where(lane_k == sub_k, g, 0.0) + jnp.where(lane_k == sub_k + batch, d, 0.0)
        red[it, me] = jnp.sum(line, axis=0, keepdims=True)

        def spread(d, c):
            t = lax.rem(me + d, ndev)
            remote(
                red.at[it, me], red.at[it, me], rsendm.at[it], rrecv.at[it],
                t // ncols, lax.rem(t, ncols),
            ).start()
            return c

        lax.fori_loop(1, ndev, spread, 0)

    def take_sums(it):
        drain(red.at[it, 0 : ndev - 1], rrecv.at[it])
        line = jnp.sum(red[it], axis=0)
        g = jnp.sum(jnp.where(lane_k == sub_k, line, 0.0), axis=1, keepdims=True)
        d = jnp.sum(jnp.where(lane_k == sub_k + batch, line, 0.0), axis=1, keepdims=True)
        return g, d

    no_edges = jnp.zeros((tile_r, 128), F32)

    r0 = rp_ref[...]
    pu0 = precond(r0)
    pl.semaphore_wait(barrier, ndev - 1)
    send_seg(0, pu0)
    loads[5].wait()

    def start(k, e):
        r = rd_ref[k]
        u = r * invd[...]
        us[0, k] = u
        gbuf[pl.ds(k, 1), :] = jnp.sum(r * u, axis=0, keepdims=True)
        return edges(0, k, u, e)

    send_edges(0, lax.fori_loop(0, batch, start, no_edges, unroll=2))
    outs = [pltpu.make_async_copy(us.at[i], us_hbm.at[i], outsem.at[i]) for i in range(ITERS)]
    outs[0].start()
    send_cont(0)
    loads[6].wait()
    high = mat_ref[...].astype(jnp.bfloat16)
    mh[...] = high
    ml[...] = (mat_ref[...] - high.astype(F32)).astype(jnp.bfloat16)

    package_product(0)
    ct0 = wait_halos(0)

    def first_image(k, e):
        u = us[0, k]
        m = image(0, k, u, ct0)
        ms[0, k] = m
        dbuf[pl.ds(k, 1), :] = jnp.sum(diag[...] * (m * u), axis=0, keepdims=True)
        return edges(1, k, m, e)

    e1 = lax.fori_loop(0, batch, first_image, no_edges)
    pw0 = package_image(0, pu0)
    pm0 = precond(pw0)
    send_seg(1, pm0)
    send_edges(1, e1)
    send_sums(0, total(gbuf, r0, pu0), total(dbuf, pw0, pu0))
    send_cont(1)

    package_product(1)
    ct1 = wait_halos(1)

    def second_image(k, c):
        ks[0, k] = image(1, k, ms[0, k], ct1)
        return c

    lax.fori_loop(0, batch, second_image, 0, unroll=2)
    pn0 = package_image(1, pm0)
    g0, d0 = take_sums(0)
    alpha0 = g0 / d0
    put(0, alpha0)
    pu1 = pu0 - alpha0 * pm0
    pw1 = pw0 - alpha0 * pn0
    r1 = r0 - alpha0 * pw0
    pm1 = precond(pw1)
    send_seg(2, pm1)

    def second_step(k, e):
        one = pl.ds(k, 1)
        a = cf[0, one, :]
        u = us[0, k] - a * ms[0, k]
        m = ms[0, k] - a * ks[0, k]
        us[1, k] = u
        ms[1, k] = m
        du = diag[...] * u
        gbuf[one, :] = jnp.sum(du * u, axis=0, keepdims=True)
        dbuf[one, :] = jnp.sum(du * m, axis=0, keepdims=True)
        return edges(2, k, m, e)

    e2 = lax.fori_loop(0, batch, second_step, no_edges, unroll=2)
    send_edges(2, e2)
    outs[1].start()
    send_sums(1, total(gbuf, r1, pu1), total(dbuf, pw1, pu1))
    send_cont(2)

    package_product(2)
    ct2 = wait_halos(2)

    def third_image(k, c):
        ks[1, k] = image(2, k, ms[1, k], ct2)
        return c

    lax.fori_loop(0, batch, third_image, 0, unroll=2)
    g1, d1 = take_sums(1)
    beta1 = g1 / g0
    alpha1 = g1 / (d1 - beta1 * g1 / alpha0)
    put(1, alpha1)
    put(2, beta1)

    def last_step(k, c):
        one = pl.ds(k, 1)
        a = cf[1, one, :]
        b = cf[2, one, :]
        m1 = ms[1, k]
        u = us[1, k] - a * (m1 + b * ms[0, k])
        m = m1 - a * (ks[1, k] + b * ks[0, k])
        us[2, k] = u
        du = diag[...] * u
        gbuf[one, :] = jnp.sum(du * u, axis=0, keepdims=True)
        dbuf[one, :] = jnp.sum(du * m, axis=0, keepdims=True)
        return c

    lax.fori_loop(0, batch, last_step, 0, unroll=2)
    pn1 = package_image(2, pm1)
    pu2 = pu1 - alpha1 * (pm1 + beta1 * pm0)
    pw2 = pw1 - alpha1 * (pn1 + beta1 * pn0)
    r2 = r1 - alpha1 * (pw1 + beta1 * pw0)
    outs[2].start()
    send_sums(2, total(gbuf, r2, pu2), total(dbuf, pw2, pu2))

    mine = me // nrows == icol
    for it in range(ITERS):
        drain(seg.at[it, 0 : ncols - 1], ssend.at[it])
        drain(cont.at[it, 0 : ncols - 1], csendm.at[it])

        @pl.when(mine)
        def _():
            drain(part.at[it, 0 : nrows - 1], psend.at[it])

        @pl.when(jnp.logical_not(mine))
        def _():
            drain(part.at[it], psend.at[it])

        for side, copy in enumerate(halos(it)):
            pl.when(has[side])(copy.wait_send)

    g2, d2 = take_sums(2)
    beta2 = g2 / g1
    c2 = g2 / (d2 - beta2 * g2 / alpha1)
    c1 = alpha1 + c2 * beta2
    c0 = alpha0 + c1 * beta1
    put(0, c0)
    put(1, c1)
    put(2, c2)
    xp_ref[...] = c0 * pu0 + c1 * pu1 + c2 * pu2
    outs.append(pltpu.make_async_copy(xp_ref, xp_hbm, outsem.at[ITERS]))
    outs.append(pltpu.make_async_copy(cf, cf_hbm, outsem.at[ITERS + 1]))
    outs[ITERS].start()
    outs[ITERS + 1].start()
    for out in outs:
        out.wait()
    for it in range(ITERS):
        drain(red.at[it, 0 : ndev - 1], rsendm.at[it])


def solution(mesh):
    nrows, ncols = mesh.shape["row"], mesh.shape["col"]

    def body(die_current, die_shunt, pkg_current, pkg_matrix, pkg_block_inv, bump_node, bump_conductance):
        batch, tile_r, tile_c = die_current.shape
        local_n = pkg_current.shape[1]
        bumps = bump_node.shape[0]
        lat_rows = bumps // BUMP_C // nrows
        lat_cols = BUMP_C // ncols
        nodes = bump_node.reshape(-1, 128)
        cond = bump_conductance.reshape(-1, 128)
        noff = len(pairs_by_offset(lat_rows, ncols, local_n))
        ndev = nrows * ncols
        vm = pltpu.VMEM
        dma = pltpu.SemaphoreType.DMA
        row = (batch, tile_c)
        us, cf, xp = pl.pallas_call(
            functools.partial(kernel, nrows, ncols, lat_rows, lat_cols),
            out_shape=(
                jax.ShapeDtypeStruct((ITERS,) + die_current.shape, F32),
                jax.ShapeDtypeStruct((ITERS,) + row, F32),
                jax.ShapeDtypeStruct(pkg_current.shape, F32),
            ),
            in_specs=[pl.BlockSpec(memory_space=pltpu.HBM)] * 7,
            out_specs=(pl.BlockSpec(memory_space=pltpu.HBM),) * 3,
            scratch_shapes=[
                vm(die_current.shape, F32),
                vm(pkg_matrix.shape, F32),
                vm(die_shunt.shape, F32),
                vm(pkg_current.shape, F32),
                vm(pkg_block_inv.shape, F32),
                vm(nodes.shape, jnp.int32),
                vm(cond.shape, F32),
                vm(pkg_current.shape, F32),
                vm((3,) + die_current.shape, F32),
                vm((2,) + die_current.shape, F32),
                vm((2,) + die_current.shape, F32),
                vm((tile_r, tile_c), F32),
                vm((tile_r, tile_c), F32),
                vm((tile_r, tile_c), F32),
                vm((tile_r, tile_c), F32),
                vm(pkg_matrix.shape, jnp.bfloat16),
                vm(pkg_matrix.shape, jnp.bfloat16),
                vm((local_n, local_n), F32),
                vm(row, F32),
                vm(row, F32),
                vm((3,) + row, F32),
                vm((lat_rows,) + row, F32),
                vm((lat_rows,) + row, F32),
                vm((noff, tile_c, local_n), jnp.bfloat16),
                vm((noff, local_n, tile_c), jnp.bfloat16),
                vm((ITERS, 2) + row, F32),
                vm((ITERS, 2) + row, F32),
                vm((ITERS, 2, batch, tile_r), F32),
                vm((ITERS, 2, batch, tile_r), F32),
                vm((ITERS, ncols, batch, local_n), F32),
                vm((ITERS, nrows, batch, local_n), F32),
                vm((ITERS, nrows, batch, local_n), F32),
                vm((ITERS, ncols, batch, local_n), F32),
                vm((ITERS, ncols, batch, local_n), F32),
                vm((ITERS, ndev, 1, 128), F32),
                dma((ITERS, 4)),
                dma((ITERS, 4)),
                dma((ITERS,)),
                dma((ITERS,)),
                dma((ITERS,)),
                dma((ITERS,)),
                dma((ITERS,)),
                dma((ITERS,)),
                dma((ITERS,)),
                dma((ITERS,)),
                dma((7,)),
                dma((ITERS + 2,)),
            ],
            compiler_params=pltpu.CompilerParams(
                collective_id=0, has_side_effects=True, vmem_limit_bytes=67043328
            ),
        )(die_current, die_shunt, pkg_current, pkg_matrix, pkg_block_inv, nodes, cond)
        scale = cf[:, :, None, :]
        xd = scale[0] * us[0] + scale[1] * us[1] + scale[2] * us[2]
        return xd, xp

    placed = (
        P(None, "row", "col"),
        P("row", "col"),
        P(None, ("row", "col")),
        P("row", "col"),
        P(("row", "col"), None, None),
        P(),
        P(),
    )
    return jax.shard_map(
        body,
        mesh=mesh,
        in_specs=placed,
        out_specs=(P(None, "row", "col"), P(None, ("row", "col"))),
        check_vma=False,
    )
```

```python
import functools

import jax
import jax.numpy as jnp
from jax import lax
from jax.experimental import pallas as pl
from jax.experimental.pallas import tpu as pltpu
from jax.sharding import PartitionSpec as P

BUMP_C = 64
PB = 32
ITERS = 3
MESH = pl.DeviceIdType.MESH
HI = lax.Precision.HIGHEST
F32 = jnp.float32


def drain(ref, sem):
    pltpu.make_async_copy(ref, ref, sem).wait()


def split3(v):
    high = v.astype(jnp.bfloat16)
    rest = v - high.astype(F32)
    mid = rest.astype(jnp.bfloat16)
    return [high, mid, (rest - mid.astype(F32)).astype(jnp.bfloat16)]


def exact_pick(parts, onehot):
    rows = sum(p.shape[0] for p in parts)
    stacked = jnp.concatenate(parts, axis=0) if len(parts) > 1 else parts[0]
    out = jnp.dot(
        jnp.concatenate(split3(stacked), axis=0), onehot, preferred_element_type=F32
    )
    return out[:rows] + out[rows : 2 * rows] + out[2 * rows :]


def pairs_by_offset(lat_rows, ncols, local_n):
    groups = {}
    for lr in range(lat_rows):
        for j in range(ncols):
            if lr * BUMP_C < (j + 1) * local_n and j * local_n < (lr + 1) * BUMP_C:
                groups.setdefault(lr * BUMP_C - j * local_n, []).append((lr, j))
    return sorted(groups.items())


def kernel(
    nrows, ncols, lat_rows, lat_cols,
    rd_hbm, shunt_hbm, rp_hbm, mat_hbm, inv_hbm, node_hbm, cond_hbm,
    xd_hbm, xp_hbm,
    rd_ref, mat_ref, shunt_ref, rp_ref, inv_ref, node_ref, cond_ref, xp_ref, us, ms, ks, diag, invd, mask, cinv, mh, ml, bd, gbuf, dbuf, cf, abuf, vpx,
    emb, embt, rsend, hr, csend, hc, seg, part, rec, cont, dat, red,
    hsend, hrecv, ssend, srecv, psend, precv, csendm, drecv, rsendm, rrecv, loadsem, outsem,
):
    ndev = nrows * ncols
    irow = lax.axis_index("row")
    icol = lax.axis_index("col")
    me = irow * ncols + icol
    batch, tile_r, tile_c = rd_ref.shape
    local_n = rp_ref.shape[1]
    cell_r = tile_r // lat_rows
    cell_c = tile_c // lat_cols
    total_c = tile_c * ncols
    groups = pairs_by_offset(lat_rows, ncols, local_n)

    loads = [
        pltpu.make_async_copy(src, dst, loadsem.at[i])
        for i, (src, dst) in enumerate(
            (
                (node_hbm, node_ref),
                (cond_hbm, cond_ref),
                (shunt_hbm, shunt_ref),
                (inv_hbm, inv_ref),
                (rp_hbm, rp_ref),
                (rd_hbm, rd_ref),
                (mat_hbm, mat_ref),
            )
        )
    ]
    for load in loads:
        load.start()

    hr[...] = jnp.zeros_like(hr)
    hc[...] = jnp.zeros_like(hc)
    barrier = pltpu.get_barrier_semaphore()

    def greet(d, c):
        t = lax.rem(me + d, ndev)
        pl.semaphore_signal(
            barrier, inc=1, device_id=(t // ncols, lax.rem(t, ncols)), device_id_type=MESH
        )
        return c

    lax.fori_loop(1, ndev, greet, 0)

    node_c = icol * lat_cols + lax.broadcasted_iota(jnp.int32, (tile_c, local_n), 0) // cell_c
    node_l = lax.broadcasted_iota(jnp.int32, (tile_c, local_n), 1)
    node_ct = icol * lat_cols + lax.broadcasted_iota(jnp.int32, (local_n, tile_c), 1) // cell_c
    node_lt = lax.broadcasted_iota(jnp.int32, (local_n, tile_c), 0)
    for g, (off, members) in enumerate(groups):
        emb[g] = jnp.where(node_c + off == node_l, 1.0, 0.0).astype(jnp.bfloat16)
        embt[g] = jnp.where(node_ct + off == node_lt, 1.0, 0.0).astype(jnp.bfloat16)
    bd[...] = jnp.zeros_like(bd)

    for load in loads[:5]:
        load.wait()
    seg_rows = lat_rows * BUMP_C // 128
    per_row = 128 // BUMP_C
    nodes = node_ref[pl.ds(irow * seg_rows, seg_rows), :]
    conds = cond_ref[pl.ds(irow * seg_rows, seg_rows), :]
    node_r = lax.rem(nodes // total_c, cell_r).astype(F32)
    node_q = lax.rem(lax.rem(nodes, total_c), cell_c).astype(F32)
    tall = jnp.concatenate([node_r, node_q, conds], axis=0)
    tall = jnp.concatenate([tall, jnp.zeros((-tall.shape[0] % 8, 128), F32)], axis=0)
    wide_l = lax.broadcasted_iota(jnp.int32, (128, tile_c), 0)
    wide_c = lax.broadcasted_iota(jnp.int32, (128, tile_c), 1) // cell_c + icol * lat_cols
    row_c = lax.broadcasted_iota(jnp.int32, (cell_r, tile_c), 0).astype(F32)
    lane_c = lax.rem(lax.broadcasted_iota(jnp.int32, (cell_r, tile_c), 1), cell_c).astype(F32)
    for q in range(per_row):
        pick = jnp.where(wide_l == wide_c + q * BUMP_C, 1.0, 0.0).astype(jnp.bfloat16)
        flat = exact_pick([tall], pick)
        for i in range(seg_rows):
            lr = i * per_row + q
            rs = slice(lr * cell_r, (lr + 1) * cell_r)
            hit = (row_c == flat[i : i + 1, :]) & (
                lane_c == flat[seg_rows + i : seg_rows + i + 1, :]
            )
            m = jnp.where(hit, 1.0, 0.0)
            cm = m * flat[2 * seg_rows + i : 2 * seg_rows + i + 1, :]
            dg = 4.0 + shunt_ref[rs, :] + cm
            iv = 1.0 / dg
            mask[rs, :] = m
            diag[rs, :] = dg
            invd[rs, :] = iv
            cinv[rs, :] = cm * iv
    first = me * local_n
    mine_l = lax.broadcasted_iota(jnp.int32, (128, local_n), 0)
    mine_n = lax.broadcasted_iota(jnp.int32, (128, local_n), 1) + lax.rem(first, 128)
    own = jnp.broadcast_to(cond_ref[pl.ds(first // 128, 1), :], (8, 128))
    chere = exact_pick([own], jnp.where(mine_l == mine_n, 1.0, 0.0).astype(jnp.bfloat16))[0:1]

    for q in range(local_n // PB):
        bd[q * PB : (q + 1) * PB, q * PB : (q + 1) * PB] = inv_ref[q]

    lane_e = lax.broadcasted_iota(jnp.int32, (tile_r, 128), 1)
    row_i = lax.broadcasted_iota(jnp.int32, (tile_r, tile_c), 0)
    lane_i = lax.broadcasted_iota(jnp.int32, (tile_r, tile_c), 1)
    sub_k = lax.broadcasted_iota(jnp.int32, (batch, 128), 0)
    lane_k = lax.broadcasted_iota(jnp.int32, (batch, 128), 1)

    def remote(src, dst, ssem, rsem, r, c):
        return pltpu.make_async_remote_copy(
            src_ref=src, dst_ref=dst, send_sem=ssem, recv_sem=rsem,
            device_id=(r, c), device_id_type=MESH,
        )

    has = (irow > 0, irow < nrows - 1, icol > 0, icol < ncols - 1)

    def halos(it):
        return (
            remote(rsend.at[it, 0], hr.at[it, 1], hsend.at[it, 0], hrecv.at[it, 1], irow - 1, icol),
            remote(rsend.at[it, 1], hr.at[it, 0], hsend.at[it, 1], hrecv.at[it, 0], irow + 1, icol),
            remote(csend.at[it, 0], hc.at[it, 1], hsend.at[it, 2], hrecv.at[it, 3], irow, icol - 1),
            remote(csend.at[it, 1], hc.at[it, 0], hsend.at[it, 3], hrecv.at[it, 2], irow, icol + 1),
        )

    def put(slot, value):
        cf[slot] = jnp.broadcast_to(value, (batch, tile_c))

    def precond(v):
        return lax.dot_general(v, bd[...], (((1,), (1,)), ((), ())), precision=HI)

    def send_seg(it, v):
        seg[it, icol] = v
        for d in range(1, ncols):
            remote(
                seg.at[it, icol], seg.at[it, icol], ssend.at[it], srecv.at[it],
                irow, lax.rem(icol + d, ncols),
            ).start()

    def edges(it, k, v, e):
        one = pl.ds(k, 1)
        rsend[it, 0, one, :] = v[0:1, :]
        rsend[it, 1, one, :] = v[tile_r - 1 : tile_r, :]
        mv = v * mask[...]
        for lr in range(lat_rows):
            abuf[lr, one, :] = jnp.sum(mv[lr * cell_r : (lr + 1) * cell_r], axis=0, keepdims=True)
        e = jnp.where(lane_e == k, v[:, 0:1], e)
        return jnp.where(lane_e == k + batch, v[:, tile_c - 1 : tile_c], e)

    def send_edges(it, e):
        et = e.T
        csend[it, 0] = et[0:batch, :]
        csend[it, 1] = et[batch : 2 * batch, :]
        for side, copy in enumerate(halos(it)):
            pl.when(has[side])(copy.start)

    def send_cont(it):
        totals = [None] * ncols
        for g, (off, members) in enumerate(groups):
            out = exact_pick([abuf[lr] for lr, j in members], emb[g])
            for i, (lr, j) in enumerate(members):
                term = out[i * batch : (i + 1) * batch]
                totals[j] = term if totals[j] is None else totals[j] + term
        for j in range(ncols):
            cont[it, j] = totals[j]
        dat[it, icol] = cont[it, icol]
        for d in range(1, ncols):
            t = lax.rem(icol + d, ncols)
            remote(
                cont.at[it, t], dat.at[it, icol], csendm.at[it], drecv.at[it], irow, t
            ).start()

    def package_product(it):
        drain(seg.at[it, 0 : ncols - 1], srecv.at[it])
        acc = None
        for j in range(ncols):
            v = seg[it, j]
            vh = v.astype(jnp.bfloat16)
            vl = (v - vh.astype(F32)).astype(jnp.bfloat16)
            span = slice(j * local_n, (j + 1) * local_n)
            both = jnp.dot(
                jnp.concatenate([vh, vl], axis=0), mh[span, :], preferred_element_type=F32
            )
            term = both[:batch] + both[batch:]
            term += jnp.dot(vh, ml[span, :], preferred_element_type=F32)
            acc = term if acc is None else acc + term
        for m in range(nrows):
            part[it, m] = acc[:, m * local_n : (m + 1) * local_n]
        for m in range(nrows):
            n = icol * nrows + m
            copy = remote(
                part.at[it, m], rec.at[it, irow], psend.at[it], precv.at[it],
                n // ncols, lax.rem(n, ncols),
            )
            pl.when(n != me)(copy.start)

            @pl.when(n == me)
            def _():
                pltpu.make_async_copy(part.at[it, m], rec.at[it, irow], precv.at[it]).start()

        totals = [None] * lat_rows
        for g, (off, members) in enumerate(groups):
            out = exact_pick([seg[it, j] for lr, j in members], embt[g])
            for i, (lr, j) in enumerate(members):
                term = out[i * batch : (i + 1) * batch]
                totals[lr] = term if totals[lr] is None else totals[lr] + term
        for lr in range(lat_rows):
            vpx[lr] = totals[lr]

    def wait_halos(it):
        for side, index in enumerate(((hr, 0), (hr, 1), (hc, 0), (hc, 1))):
            ref, pos = index

            @pl.when(has[side])
            def _():
                drain(ref.at[it, pos], hrecv.at[it, side])

        return jnp.concatenate(
            [hc[it, 0], hc[it, 1], jnp.zeros((128 - 2 * batch, tile_r), F32)], axis=0
        ).T

    def image(it, k, v, ct):
        one = pl.ds(k, 1)
        left = jnp.sum(jnp.where(lane_e == k, ct, 0.0), axis=1, keepdims=True)
        right = jnp.sum(jnp.where(lane_e == k + batch, ct, 0.0), axis=1, keepdims=True)
        near = jnp.where(row_i == 0, hr[it, 0, one, :], pltpu.roll(v, 1, 0))
        near += jnp.where(row_i == tile_r - 1, hr[it, 1, one, :], pltpu.roll(v, tile_r - 1, 0))
        near += jnp.where(lane_i == 0, left, pltpu.roll(v, 1, 1))
        near += jnp.where(lane_i == tile_c - 1, right, pltpu.roll(v, tile_c - 1, 1))
        feed = jnp.concatenate(
            [
                cinv[lr * cell_r : (lr + 1) * cell_r, :] * vpx[lr, one, :]
                for lr in range(lat_rows)
            ],
            axis=0,
        )
        return v - near * invd[...] - feed

    def package_image(it, v):
        drain(rec.at[it], precv.at[it])
        drain(dat.at[it, 0 : ncols - 1], drecv.at[it])
        out = rec[it, 0]
        for i in range(1, nrows):
            out += rec[it, i]
        die_at = dat[it, 0]
        for j in range(1, ncols):
            die_at += dat[it, j]
        return out + chere * (v - die_at)

    def total(buf, a, b):
        return jnp.sum(buf[...], axis=1, keepdims=True) + jnp.sum(a * b, axis=1, keepdims=True)

    def send_sums(it, g, d):
        line = jnp.where(lane_k == sub_k, g, 0.0) + jnp.where(lane_k == sub_k + batch, d, 0.0)
        red[it, me] = jnp.sum(line, axis=0, keepdims=True)

        def spread(d, c):
            t = lax.rem(me + d, ndev)
            remote(
                red.at[it, me], red.at[it, me], rsendm.at[it], rrecv.at[it],
                t // ncols, lax.rem(t, ncols),
            ).start()
            return c

        lax.fori_loop(1, ndev, spread, 0)

    def take_sums(it):
        drain(red.at[it, 0 : ndev - 1], rrecv.at[it])
        line = jnp.sum(red[it], axis=0)
        g = jnp.sum(jnp.where(lane_k == sub_k, line, 0.0), axis=1, keepdims=True)
        d = jnp.sum(jnp.where(lane_k == sub_k + batch, line, 0.0), axis=1, keepdims=True)
        return g, d

    no_edges = jnp.zeros((tile_r, 128), F32)

    r0 = rp_ref[...]
    pu0 = precond(r0)
    pl.semaphore_wait(barrier, ndev - 1)
    send_seg(0, pu0)
    loads[5].wait()

    def start(k, e):
        r = rd_ref[k]
        u = r * invd[...]
        us[0, k] = u
        gbuf[pl.ds(k, 1), :] = jnp.sum(r * u, axis=0, keepdims=True)
        return edges(0, k, u, e)

    send_edges(0, lax.fori_loop(0, batch, start, no_edges, unroll=2))
    send_cont(0)
    loads[6].wait()
    high = mat_ref[...].astype(jnp.bfloat16)
    mh[...] = high
    ml[...] = (mat_ref[...] - high.astype(F32)).astype(jnp.bfloat16)

    package_product(0)
    ct0 = wait_halos(0)

    def first_image(k, e):
        u = us[0, k]
        m = image(0, k, u, ct0)
        ms[0, k] = m
        dbuf[pl.ds(k, 1), :] = jnp.sum(diag[...] * (m * u), axis=0, keepdims=True)
        return edges(1, k, m, e)

    e1 = lax.fori_loop(0, batch, first_image, no_edges)
    pw0 = package_image(0, pu0)
    pm0 = precond(pw0)
    send_seg(1, pm0)
    send_edges(1, e1)
    send_sums(0, total(gbuf, r0, pu0), total(dbuf, pw0, pu0))
    send_cont(1)

    package_product(1)
    ct1 = wait_halos(1)

    def second_image(k, c):
        ks[0, k] = image(1, k, ms[0, k], ct1)
        return c

    lax.fori_loop(0, batch, second_image, 0, unroll=2)
    pn0 = package_image(1, pm0)
    g0, d0 = take_sums(0)
    alpha0 = g0 / d0
    put(0, alpha0)
    pu1 = pu0 - alpha0 * pm0
    pw1 = pw0 - alpha0 * pn0
    r1 = r0 - alpha0 * pw0
    pm1 = precond(pw1)
    send_seg(2, pm1)

    def second_step(k, e):
        one = pl.ds(k, 1)
        a = cf[0, one, :]
        u = us[0, k] - a * ms[0, k]
        m = ms[0, k] - a * ks[0, k]
        us[1, k] = u
        ms[1, k] = m
        du = diag[...] * u
        gbuf[one, :] = jnp.sum(du * u, axis=0, keepdims=True)
        dbuf[one, :] = jnp.sum(du * m, axis=0, keepdims=True)
        return edges(2, k, m, e)

    e2 = lax.fori_loop(0, batch, second_step, no_edges, unroll=2)
    send_edges(2, e2)
    send_sums(1, total(gbuf, r1, pu1), total(dbuf, pw1, pu1))
    send_cont(2)

    package_product(2)
    ct2 = wait_halos(2)

    def third_image(k, c):
        ks[1, k] = image(2, k, ms[1, k], ct2)
        return c

    lax.fori_loop(0, batch, third_image, 0, unroll=2)
    g1, d1 = take_sums(1)
    beta1 = g1 / g0
    alpha1 = g1 / (d1 - beta1 * g1 / alpha0)
    put(1, alpha1)
    put(2, beta1)

    def last_step(k, c):
        one = pl.ds(k, 1)
        a = cf[1, one, :]
        b = cf[2, one, :]
        m1 = ms[1, k]
        u = us[1, k] - a * (m1 + b * ms[0, k])
        m = m1 - a * (ks[1, k] + b * ks[0, k])
        us[2, k] = u
        du = diag[...] * u
        gbuf[one, :] = jnp.sum(du * u, axis=0, keepdims=True)
        dbuf[one, :] = jnp.sum(du * m, axis=0, keepdims=True)
        return c

    lax.fori_loop(0, batch, last_step, 0, unroll=2)
    pn1 = package_image(2, pm1)
    pu2 = pu1 - alpha1 * (pm1 + beta1 * pm0)
    pw2 = pw1 - alpha1 * (pn1 + beta1 * pn0)
    r2 = r1 - alpha1 * (pw1 + beta1 * pw0)
    send_sums(2, total(gbuf, r2, pu2), total(dbuf, pw2, pu2))

    mine = me // nrows == icol
    for it in range(ITERS):
        drain(seg.at[it, 0 : ncols - 1], ssend.at[it])
        drain(cont.at[it, 0 : ncols - 1], csendm.at[it])

        @pl.when(mine)
        def _():
            drain(part.at[it, 0 : nrows - 1], psend.at[it])

        @pl.when(jnp.logical_not(mine))
        def _():
            drain(part.at[it], psend.at[it])

        for side, copy in enumerate(halos(it)):
            pl.when(has[side])(copy.wait_send)

    g2, d2 = take_sums(2)
    beta2 = g2 / g1
    c2 = g2 / (d2 - beta2 * g2 / alpha1)
    c1 = alpha1 + c2 * beta2
    c0 = alpha0 + c1 * beta1
    put(0, c0)
    put(1, c1)
    put(2, c2)
    xp_ref[...] = c0 * pu0 + c1 * pu1 + c2 * pu2
    xp_out = pltpu.make_async_copy(xp_ref, xp_hbm, outsem.at[0])
    xp_out.start()

    def finish(k, c):
        one = pl.ds(k, 1)
        rd_ref[k] = cf[0, one, :] * us[0, k] + cf[1, one, :] * us[1, k] + cf[2, one, :] * us[2, k]
        pltpu.make_async_copy(rd_ref.at[k], xd_hbm.at[k], outsem.at[1]).start()
        return c

    lax.fori_loop(0, batch, finish, 0)
    xp_out.wait()
    pltpu.make_async_copy(rd_ref, xd_hbm, outsem.at[1]).wait()
    for it in range(ITERS):
        drain(red.at[it, 0 : ndev - 1], rsendm.at[it])


def deliver(x_hbm, p_hbm, xo_hbm, po_hbm, buf, pbuf, insem, outsem):
    batch = buf.shape[0]
    steps = [(x_hbm.at[k], buf.at[k], xo_hbm.at[k]) for k in range(batch)]
    steps.append((p_hbm, pbuf, po_hbm))
    ins = [pltpu.make_async_copy(a, b, insem.at[i]) for i, (a, b, c) in enumerate(steps)]
    outs = [pltpu.make_async_copy(b, c, outsem.at[i]) for i, (a, b, c) in enumerate(steps)]
    for copy in ins:
        copy.start()
    for load, store in zip(ins, outs):
        load.wait()
        store.start()
    for copy in outs:
        copy.wait()


def solution(mesh):
    nrows, ncols = mesh.shape["row"], mesh.shape["col"]

    def body(die_current, die_shunt, pkg_current, pkg_matrix, pkg_block_inv, bump_node, bump_conductance):
        batch, tile_r, tile_c = die_current.shape
        local_n = pkg_current.shape[1]
        bumps = bump_node.shape[0]
        lat_rows = bumps // BUMP_C // nrows
        lat_cols = BUMP_C // ncols
        nodes = bump_node.reshape(-1, 128)
        cond = bump_conductance.reshape(-1, 128)
        noff = len(pairs_by_offset(lat_rows, ncols, local_n))
        ndev = nrows * ncols
        vm = pltpu.VMEM
        dma = pltpu.SemaphoreType.DMA
        row = (batch, tile_c)
        xd, xp = pl.pallas_call(
            functools.partial(kernel, nrows, ncols, lat_rows, lat_cols),
            out_shape=(
                jax.ShapeDtypeStruct(die_current.shape, F32),
                jax.ShapeDtypeStruct(pkg_current.shape, F32),
            ),
            in_specs=[pl.BlockSpec(memory_space=pltpu.HBM)] * 7,
            out_specs=(pl.BlockSpec(memory_space=pltpu.HBM),) * 2,
            scratch_shapes=[
                vm(die_current.shape, F32),
                vm(pkg_matrix.shape, F32),
                vm(die_shunt.shape, F32),
                vm(pkg_current.shape, F32),
                vm(pkg_block_inv.shape, F32),
                vm(nodes.shape, jnp.int32),
                vm(cond.shape, F32),
                vm(pkg_current.shape, F32),
                vm((3,) + die_current.shape, F32),
                vm((2,) + die_current.shape, F32),
                vm((2,) + die_current.shape, F32),
                vm((tile_r, tile_c), F32),
                vm((tile_r, tile_c), F32),
                vm((tile_r, tile_c), F32),
                vm((tile_r, tile_c), F32),
                vm(pkg_matrix.shape, jnp.bfloat16),
                vm(pkg_matrix.shape, jnp.bfloat16),
                vm((local_n, local_n), F32),
                vm(row, F32),
                vm(row, F32),
                vm((3,) + row, F32),
                vm((lat_rows,) + row, F32),
                vm((lat_rows,) + row, F32),
                vm((noff, tile_c, local_n), jnp.bfloat16),
                vm((noff, local_n, tile_c), jnp.bfloat16),
                vm((ITERS, 2) + row, F32),
                vm((ITERS, 2) + row, F32),
                vm((ITERS, 2, batch, tile_r), F32),
                vm((ITERS, 2, batch, tile_r), F32),
                vm((ITERS, ncols, batch, local_n), F32),
                vm((ITERS, nrows, batch, local_n), F32),
                vm((ITERS, nrows, batch, local_n), F32),
                vm((ITERS, ncols, batch, local_n), F32),
                vm((ITERS, ncols, batch, local_n), F32),
                vm((ITERS, ndev, 1, 128), F32),
                dma((ITERS, 4)),
                dma((ITERS, 4)),
                dma((ITERS,)),
                dma((ITERS,)),
                dma((ITERS,)),
                dma((ITERS,)),
                dma((ITERS,)),
                dma((ITERS,)),
                dma((ITERS,)),
                dma((ITERS,)),
                dma((7,)),
                dma((2,)),
            ],
            compiler_params=pltpu.CompilerParams(
                collective_id=0, has_side_effects=True, vmem_limit_bytes=67043328
            ),
        )(die_current, die_shunt, pkg_current, pkg_matrix, pkg_block_inv, nodes, cond)
        return pl.pallas_call(
            deliver,
            out_shape=(
                jax.ShapeDtypeStruct(xd.shape, F32),
                jax.ShapeDtypeStruct(xp.shape, F32),
            ),
            in_specs=[pl.BlockSpec(memory_space=pltpu.HBM)] * 2,
            out_specs=(pl.BlockSpec(memory_space=pltpu.HBM),) * 2,
            scratch_shapes=[
                vm(xd.shape, F32),
                vm(xp.shape, F32),
                dma((batch + 1,)),
                dma((batch + 1,)),
            ],
            compiler_params=pltpu.CompilerParams(vmem_limit_bytes=67043328),
        )(xd, xp)

    placed = (
        P(None, "row", "col"),
        P("row", "col"),
        P(None, ("row", "col")),
        P("row", "col"),
        P(("row", "col"), None, None),
        P(),
        P(),
    )
    return jax.shard_map(
        body,
        mesh=mesh,
        in_specs=placed,
        out_specs=(P(None, "row", "col"), P(None, ("row", "col"))),
        check_vma=False,
    )
```
